512 devices in a mesh: region: 16 (over y, x), tile: 32 (over z, core).
Axes of the slice: x: 4, y: 4, z: 16, core: 2. Of those that a mesh axis runs over, the one named last changes fastest.
Arguments:
- density: float32 [16, 1024, 1024], P('region', 'tile'), may hold values from -48 to 56, as said below
- atom_xyz: float32 [16, 3, 256], P('region'), may hold values from 0 to 3
- atom_of: int32 [16, 1024], P('region'), may hold values from 0 to 255
- exponent: float32 [16, 1024], P('region'), may hold values from 0.1 to 1
- points: float32 [1024, 3, 512], P(('region', 'tile')), may hold values from 0 to 3
- weights: float32 [1024, 512], P(('region', 'tile')), may hold values from 6.1035156e-05 to 0.00018310547
- lists: int32 [1024, 4], P(('region', 'tile')), may hold values from 0 to 7, all different within a row
- live: int32 [512], P(('region', 'tile')), may hold values from 1 to 2, as said below
Outputs:
- potential: float32 [16, 1024, 1024], P('region', 'tile')
The draws below stay inside these ranges and needn't reach their ends.
Inputs may be any that keep to these rules, and one draw needn't show every extreme that they name: `density`: each region's matrix is symmetric and positive definite. `lists`: each row names 4 different blocks of its own region. a device's slots 0 to live - 1 hold its live batches and the others are unused; some device has 2.
All inputs are finite; a program needn't handle non-finite values.
Results may differ from the reference program's by a relative error of at most 0.0003.
Values sent between devices are 32-bit elements; how exact they have to be, the bound alone decides.
No kernel may reach another device: no remote copies, remote signals or barrier semaphores. Data moves between devices by JAX's collectives and lax.ppermute only.
A program may use at most 128 MiB of HBM per device.

```python
import math
import jax
import jax.numpy as jnp
from jax import lax

NFR = 1024
BLK = 128
NBLK = 4
P_SIZE = 512
NATOM = 256
BPD = 2
NBAT = 1024
N_REGION = 16
N_TILE = 32


def draw_density(key, part):
    key_factor, key_diag = jax.random.split(jax.random.fold_in(key, 7), 2)
    factor_cols = NFR // 4
    half_width = math.sqrt(3.0)
    factor = jax.random.uniform(key_factor, (N_REGION, NFR, factor_cols), jnp.float32, -half_width, half_width)
    gram_matrix = jnp.einsum('rik,rjk->rij', factor, factor, precision=lax.Precision.HIGHEST) / factor_cols
    gram_matrix = 0.5 * (gram_matrix + jnp.swapaxes(gram_matrix, 1, 2))
    identity = jnp.eye(NFR, dtype=jnp.float32)[None]
    diag_shift = jax.random.uniform(key_diag, (N_REGION, NFR), jnp.float32, 0.1, 0.5)
    matrix = gram_matrix + identity * diag_shift[:, :, None]
    return matrix


def draw_live(key, part):
    key_level, key_jitter, key_pick = jax.random.split(jax.random.fold_in(key, 13), 3)
    region_level = jax.random.randint(key_level, (N_REGION, 1), 1, BPD + 1)
    jitter = jax.random.randint(key_jitter, (N_REGION, N_TILE), -1, 2)
    counts = jnp.clip(region_level + jitter, 1, BPD).reshape(-1)
    chosen = jax.random.randint(key_pick, (), 0, N_REGION * N_TILE)
    return jnp.where(jnp.arange(N_REGION * N_TILE) == chosen, BPD, counts).astype(jnp.int32)


def set_ends(drawn, key, smallest, largest):
    shape = drawn.shape
    place = [jax.random.randint(jax.random.fold_in(key, axis), (), 0, shape[axis]) for axis in range(len(shape))]
    drawn = drawn.at[tuple(place)].set(smallest)
    longest = shape.index(max(shape))
    place[longest] = (place[longest] + 1) % shape[longest]
    return drawn.at[tuple(place)].set(largest)


def steps_of(stream_key, dims, cuts, smallest, high):
    factor_of = 1.0
    for position, shards_of in cuts:
        heights = jax.random.uniform(jax.random.fold_in(jax.random.fold_in(stream_key, 6), position), (shards_of,), jnp.float32, smallest / len(cuts), high / len(cuts))
        factor_of = factor_of * jnp.repeat(jnp.exp(heights), dims[position] // shards_of).reshape((-1,) + (1,) * (len(dims) - 1 - position))
    return factor_of


def choose_distinct(key, rows, count, top, lift):
    ranking = jax.random.permutation(jax.random.fold_in(key, 1), count)
    boost = ranking
    for power in range(3):
        boost = boost * boost // count
    boost = boost * lift // count
    lots = jax.random.randint(jax.random.fold_in(key, 2), (rows, count), 0, 4096) + boost
    sure = jax.random.permutation(jax.random.fold_in(key, 3), rows)[jnp.arange(count) % rows]
    lots = jnp.where(jnp.arange(rows)[:, None] == sure[None, :], 1 << 14, lots)
    priority = lots * count + jnp.arange(count)
    return lax.top_k(priority.astype(jnp.int32), top)[1].astype(jnp.int32)


def setup_inputs(seed: int = 0) -> dict:
    seeds = jax.random.split(jax.random.key(seed), 9)
    density = draw_density(jax.random.fold_in(seeds[8], 71), 0)
    atom_xyz = jnp.clip(3.0 * jax.random.uniform(seeds[1], (N_REGION, 3, NATOM), jnp.float32) ** steps_of(seeds[1], (N_REGION, 3, NATOM), ((0, 16),), -0.2, 0.2), 0.0, 3.0)
    atom_of = set_ends(jax.random.randint(seeds[2], (N_REGION, NFR), 0, NATOM), jax.random.fold_in(seeds[2], 1), 0, NATOM - 1).astype(jnp.int32)
    exponent = jnp.clip(jnp.exp(math.log(1.0) - 2.3025851 * jax.random.uniform(seeds[3], (N_REGION, NFR), jnp.float32) ** steps_of(seeds[3], (N_REGION, NFR), ((0, 16),), -0.2, 0.2)), 0.1, 1.0)
    points = jnp.clip(3.0 * jax.random.uniform(seeds[4], (NBAT, 3, P_SIZE), jnp.float32) ** steps_of(seeds[4], (NBAT, 3, P_SIZE), ((0, 512),), -0.2, 0.2), 0.0, 3.0)
    weights = jnp.clip(6.103515625e-05 + 0.00012207031 * jax.random.uniform(seeds[5], (NBAT, P_SIZE), jnp.float32) ** steps_of(seeds[5], (NBAT, P_SIZE), ((0, 512),), -0.2, 0.2), 6.103515625e-05, 0.00018310547)
    lists = choose_distinct(seeds[6], NBAT, NFR // BLK, NBLK, 0)
    live = draw_live(jax.random.fold_in(seeds[8], 71), 0)
    return dict(density=density, atom_xyz=atom_xyz, atom_of=atom_of, exponent=exponent, points=points, weights=weights, lists=lists, live=live)


slater_coef = (3.0 / math.pi) ** (1.0 / 3.0)
highest = lax.Precision.HIGHEST


def expand_blocks(blocks):
    inner = jnp.arange(BLK, dtype=jnp.int32)
    full = blocks[..., :, None] * BLK + inner
    return full.reshape(blocks.shape[:-1] + (blocks.shape[-1] * BLK,))


def gather_block(region_density, blocks):
    block_total = region_density.shape[0] // BLK
    count = blocks.shape[0]
    tiled = region_density.reshape(block_total, BLK, block_total, BLK)
    picked = jnp.take(jnp.take(tiled, blocks, axis=0), blocks, axis=2)
    return picked.reshape(count * BLK, count * BLK)


def add_term(running, blocks, batch_result):
    block_total = running.shape[0] // BLK
    count = blocks.shape[0]
    tiled = running.reshape(block_total, BLK, block_total, BLK)
    update = jnp.transpose(batch_result.reshape(count, BLK, count, BLK), (0, 2, 1, 3))
    tiled = tiled.at[blocks[:, None], :, blocks[None, :], :].add(update)
    return tiled.reshape(running.shape)


def batch_term(coords, weight, centers, exponents, block_density):
    distance = jnp.zeros((coords.shape[1], centers.shape[1]), jnp.float32)
    for axis_no in range(3):
        offset = coords[axis_no][:, None] - centers[axis_no][None, :]
        distance = distance + offset * offset
    orbital = jnp.exp(-exponents[None, :] * distance)
    mixed = jnp.dot(orbital, block_density, precision=highest, preferred_element_type=jnp.float32)
    point_density = jnp.sum(orbital * mixed, axis=1)
    factor = weight * (-slater_coef) * jnp.cbrt(point_density)
    return lax.dot_general(orbital, orbital * factor[:, None], (((0,), (0,)), ((), ())), precision=highest, preferred_element_type=jnp.float32)


def region_potential(inputs):
    density_block, table_xyz, atom_index, exponent_row, region_points, region_weights, region_lists, alive_mask = inputs

    def visit_batch(running, batch_inputs):
        coords, weight, blocks, is_alive = batch_inputs
        members = expand_blocks(blocks)
        centers = jnp.take(table_xyz, jnp.take(atom_index, members), axis=1)
        exponents = jnp.take(exponent_row, members)
        block_density = gather_block(density_block, blocks)

        def compute(running):
            return add_term(running, blocks, batch_term(coords, weight, centers, exponents, block_density))

        running = lax.cond(is_alive > 0, compute, lambda running: running, running)
        return running, None

    running = jnp.zeros((NFR, NFR), jnp.float32)
    running, _ = lax.scan(visit_batch, running, (region_points, region_weights, region_lists, alive_mask))
    return running


def reference(density, atom_xyz, atom_of, exponent, points, weights, lists, live):
    per_region = N_TILE * BPD
    slot_index = jnp.arange(per_region, dtype=jnp.int32) % BPD
    live_grid = jnp.repeat(live.reshape(N_REGION, N_TILE), BPD, axis=1)
    alive_mask = (slot_index[None, :] < live_grid).astype(jnp.int32)
    region_points = points.reshape(N_REGION, per_region, 3, P_SIZE)
    region_weights = weights.reshape(N_REGION, per_region, P_SIZE)
    region_lists = lists.reshape(N_REGION, per_region, NBLK)
    return lax.map(region_potential, (density, atom_xyz, atom_of, exponent, region_points, region_weights, region_lists, alive_mask))
```

```python
import math

import jax
import jax.numpy as jnp
from jax import lax
from jax.experimental import pallas as pl
from jax.experimental.pallas import tpu as pltpu
from jax.sharding import Mesh
from jax.sharding import PartitionSpec as P

BLK = 128
NBLK = 4
PTS = 512
NF = 1024
OWNERS = 8
SLOTS = 16
PACK = 640
TILE = ("zh", "zl", "core")
ALL = ("region", "zh", "zl", "core")
SWAP = [(0, 1), (1, 0)]
FLIP = [(0, 3), (1, 2), (2, 1), (3, 0)]

slater_coef = (3.0 / math.pi) ** (1.0 / 3.0)


def split(x):
    hi = x.astype(jnp.bfloat16)
    lo = (x - hi.astype(jnp.float32)).astype(jnp.bfloat16)
    return hi, lo


def dot_nn(a, b):
    return lax.dot_general(a, b, (((1,), (0,)), ((), ())), preferred_element_type=jnp.float32)


def dot_nt(a, b):
    return lax.dot_general(a, b, (((1,), (1,)), ((), ())), preferred_element_type=jnp.float32)


def build_table(xyz_ref, atom_ref, exp_ref, cen):
    atoms = lax.broadcasted_iota(jnp.int32, (256, NF), 0)
    picked = jnp.where(atoms == atom_ref[...], 1.0, 0.0).astype(jnp.float32)
    rows = jnp.concatenate([xyz_ref[...], jnp.zeros((5, 256), jnp.float32)], axis=0)
    centers = jnp.dot(rows, picked, precision=lax.Precision.HIGHEST, preferred_element_type=jnp.float32)
    row_no = lax.broadcasted_iota(jnp.int32, (8, NF), 0)
    table = jnp.where(row_no == 3, -exp_ref[...], centers)
    columns = jnp.transpose(table)
    for c in range(4):
        cen[c] = jnp.broadcast_to(columns[:, c : c + 1], (NF, BLK))


def active_list(lists_ref, own, order):
    def visit(b, n):
        named = lists_ref[b * 4] == own
        for j in range(1, NBLK):
            named = jnp.logical_or(named, lists_ref[b * 4 + j] == own)
        order[n] = b
        return n + named.astype(jnp.int32)

    return lax.fori_loop(0, SLOTS, visit, 0)


def position(lists_ref, b, own):
    at = jnp.int32(0)
    for j in range(1, NBLK):
        at = jnp.where(lists_ref[b * 4 + j] == own, j, at)
    return at


def fill_phi(lists_ref, grid_ref, b, cen, phi_hi, phi_lo):
    rows = [grid_ref[pl.ds(b * 4 + c, 1), 0:PTS] for c in range(3)]
    step = 32
    for j in range(NBLK):
        base = pl.multiple_of(lists_ref[b * 4 + j] * BLK, BLK)
        for r in range(0, BLK, step):
            at = pl.ds(base + r, step)
            center = [cen[c, at, :] for c in range(4)]
            for t in range(0, PTS, BLK):
                dx = rows[0][:, t : t + BLK] - center[0]
                dy = rows[1][:, t : t + BLK] - center[1]
                dz = rows[2][:, t : t + BLK] - center[2]
                dist = dx * dx + dy * dy + dz * dz
                hi, lo = split(jnp.exp(center[3] * dist))
                phi_hi[j * BLK + r : j * BLK + r + step, t : t + BLK] = hi
                phi_lo[j * BLK + r : j * BLK + r + step, t : t + BLK] = lo


def own_phi(at, phi_hi, phi_lo):
    where = pl.ds(pl.multiple_of(at * BLK, BLK), BLK)
    return phi_hi[where, :].astype(jnp.float32) + phi_lo[where, :].astype(jnp.float32)


def rho_kernel(lists_ref, grid_ref, d0, d1, d2, d3, xyz_ref, atom_ref, exp_ref, rho_ref, cen, dens, phi_hi, phi_lo, order):
    own = lax.axis_index("zh")
    piece = lax.axis_index("zl") * 2 + lax.axis_index("core")
    build_table(xyz_ref, atom_ref, exp_ref, cen)
    for i, ref in enumerate((d0, d1, d2, d3)):
        hi, lo = split(ref[...])
        at = pl.multiple_of((piece ^ i) * 32, 32)
        dens[pl.ds(at, 32), :] = hi
        dens[pl.ds(at + BLK, 32), :] = lo
    rho_ref[...] = jnp.zeros_like(rho_ref)
    count = active_list(lists_ref, own, order)

    def visit(i, carry):
        b = order[i]
        fill_phi(lists_ref, grid_ref, b, cen, phi_hi, phi_lo)
        mixed = jnp.zeros((BLK, PTS), jnp.float32)
        for j in range(0, NBLK, 2):
            cols = [pl.ds(pl.multiple_of(lists_ref[b * 4 + j + k] * BLK, BLK), BLK) for k in range(2)]
            pair = jnp.concatenate([dens[:, cols[0]], dens[:, cols[1]]], axis=1)
            rows = slice(j * BLK, (j + 2) * BLK)
            both = dot_nn(pair, phi_hi[rows, :])
            mixed = mixed + both[:BLK] + both[BLK:] + dot_nn(pair[:BLK], phi_lo[rows, :])
        mine = own_phi(position(lists_ref, b, own), phi_hi, phi_lo)
        rho_ref[pl.ds(b, 1), :] = jnp.sum(mine * mixed, axis=0, keepdims=True)
        return carry

    lax.fori_loop(0, count, visit, 0)


def cube_root(x):
    size = jnp.abs(x)
    safe = jnp.maximum(size, 1e-37)
    y = jnp.exp(jnp.log(safe) * (1.0 / 3.0))
    y = y - (y - safe / (y * y)) * (1.0 / 3.0)
    y = jnp.where(size < 1e-37, 0.0, y)
    return jnp.where(x < 0.0, -y, y)


def matrix_kernel(lists_ref, grid_ref, parts_ref, xyz_ref, atom_ref, exp_ref, v0, v1, v2, v3, cen, total, root, phi_hi, phi_lo, order):
    own = lax.axis_index("zh")
    piece = lax.axis_index("zl") * 2 + lax.axis_index("core")
    build_table(xyz_ref, atom_ref, exp_ref, cen)
    rho = parts_ref[0]
    for k in range(1, OWNERS):
        rho = rho + parts_ref[k]
    root[...] = cube_root(rho) * (-slater_coef)
    total[...] = jnp.zeros_like(total)
    count = active_list(lists_ref, own, order)

    def visit(i, carry):
        b = order[i]
        fill_phi(lists_ref, grid_ref, b, cen, phi_hi, phi_lo)
        factor = grid_ref[pl.ds(b * 4 + 3, 1), 0:PTS] * root[pl.ds(b, 1), :]
        mine = own_phi(position(lists_ref, b, own), phi_hi, phi_lo)
        hi, lo = split(mine * factor)
        pair = jnp.concatenate([hi, lo], axis=0)
        both = dot_nt(pair, phi_hi[...])
        result = both[:BLK] + both[BLK:] + dot_nt(hi, phi_lo[...])
        for j in range(NBLK):
            cols = pl.ds(pl.multiple_of(lists_ref[b * 4 + j] * BLK, BLK), BLK)
            total[:, cols] += result[:, j * BLK : (j + 1) * BLK]
        return carry

    lax.fori_loop(0, count, visit, 0)
    for i, ref in enumerate((v0, v1, v2, v3)):
        at = pl.multiple_of((piece ^ i) * 32, 32)
        ref[...] = total[pl.ds(at, 32), :]


smem = pl.BlockSpec(memory_space=pltpu.SMEM)
vmem = pl.BlockSpec(memory_space=pltpu.VMEM)


def body(density, atom_xyz, atom_of, exponent, points, weights, lists, live):
    own_rows = density[0]
    others = (
        lax.ppermute(own_rows, "core", SWAP),
        lax.ppermute(own_rows, "zl", SWAP),
        lax.ppermute(own_rows, ("zl", "core"), FLIP),
    )
    slot_no = jnp.arange(2, dtype=jnp.int32)
    named = jnp.where(slot_no[:, None] < live[0], lists, -1).astype(jnp.float32)
    grid = jnp.concatenate([points, weights[:, None, :]], axis=1)
    extra = jnp.broadcast_to(jnp.pad(named, ((0, 0), (0, PACK - PTS - NBLK)))[:, None, :], (2, 4, PACK - PTS))
    packed = jnp.concatenate([grid, extra], axis=2).reshape(8, PACK)
    gathered = lax.all_to_all(jnp.broadcast_to(packed[None], (OWNERS, 8, PACK)), "zh", 0, 0)
    all_lists = gathered.reshape(SLOTS, 4, PACK)[:, 0, PTS : PTS + NBLK].astype(jnp.int32).reshape(SLOTS * NBLK)
    gathered = gathered.reshape(SLOTS * 4, PACK)
    local = (atom_xyz[0], atom_of, exponent)
    rho = pl.pallas_call(
        rho_kernel,
        out_shape=jax.ShapeDtypeStruct((SLOTS, PTS), jnp.float32),
        in_specs=[smem] + [vmem] * 8,
        out_specs=vmem,
        scratch_shapes=[
            pltpu.VMEM((4, NF, BLK), jnp.float32),
            pltpu.VMEM((2 * BLK, NF), jnp.bfloat16),
            pltpu.VMEM((PTS, PTS), jnp.bfloat16),
            pltpu.VMEM((PTS, PTS), jnp.bfloat16),
            pltpu.SMEM((SLOTS + 1,), jnp.int32),
        ],
        name="rho",
    )(all_lists, gathered, own_rows, *others, *local)
    parts = lax.all_to_all(jnp.broadcast_to(rho[None], (OWNERS, SLOTS, PTS)), "zh", 0, 0)
    pieces = pl.pallas_call(
        matrix_kernel,
        out_shape=[jax.ShapeDtypeStruct((32, NF), jnp.float32)] * 4,
        in_specs=[smem] + [vmem] * 5,
        out_specs=[vmem] * 4,
        scratch_shapes=[
            pltpu.VMEM((4, NF, BLK), jnp.float32),
            pltpu.VMEM((BLK, NF), jnp.float32),
            pltpu.VMEM((SLOTS, PTS), jnp.float32),
            pltpu.VMEM((PTS, PTS), jnp.bfloat16),
            pltpu.VMEM((PTS, PTS), jnp.bfloat16),
            pltpu.SMEM((SLOTS + 1,), jnp.int32),
        ],
        name="matrix",
    )(all_lists, gathered, parts, *local)
    total = (
        pieces[0]
        + lax.ppermute(pieces[1], "core", SWAP)
        + lax.ppermute(pieces[2], "zl", SWAP)
        + lax.ppermute(pieces[3], ("zl", "core"), FLIP)
    )
    return total[None]


def solution(mesh):
    torus = Mesh(mesh.devices.reshape(mesh.shape["region"], OWNERS, 2, 2), ALL)
    return jax.shard_map(
        body,
        mesh=torus,
        in_specs=(
            P("region", TILE, None),
            P("region", None, None),
            P("region", None),
            P("region", None),
            P(ALL, None, None),
            P(ALL, None),
            P(ALL, None),
            P(ALL),
        ),
        out_specs=P("region", TILE, None),
        check_vma=False,
    )
```

```python
import math

import jax
import jax.numpy as jnp
from jax import lax
from jax.experimental import pallas as pl
from jax.experimental.pallas import tpu as pltpu
from jax.sharding import Mesh
from jax.sharding import PartitionSpec as P

BLK = 128
NBLK = 4
PTS = 512
NF = 1024
OWNERS = 8
SLOTS = 16
PACK = 640
TILE = ("zh", "zl", "core")
ALL = ("region", "zh", "zl", "core")
SWAP = [(0, 1), (1, 0)]
FLIP = [(0, 3), (1, 2), (2, 1), (3, 0)]

slater_coef = (3.0 / math.pi) ** (1.0 / 3.0)


def split(x):
    hi = x.astype(jnp.bfloat16)
    lo = (x - hi.astype(jnp.float32)).astype(jnp.bfloat16)
    return hi, lo


def dot_nn(a, b):
    return lax.dot_general(a, b, (((1,), (0,)), ((), ())), preferred_element_type=jnp.float32)


def dot_nt(a, b):
    return lax.dot_general(a, b, (((1,), (1,)), ((), ())), preferred_element_type=jnp.float32)


def build_table(xyz_ref, atom_ref, exp_ref, cen):
    atoms = lax.broadcasted_iota(jnp.int32, (256, NF), 0)
    picked = jnp.where(atoms == atom_ref[...], 1.0, 0.0).astype(jnp.float32)
    rows = jnp.concatenate([xyz_ref[...], jnp.zeros((5, 256), jnp.float32)], axis=0)
    centers = jnp.dot(rows, picked, precision=lax.Precision.HIGHEST, preferred_element_type=jnp.float32)
    row_no = lax.broadcasted_iota(jnp.int32, (8, NF), 0)
    table = jnp.where(row_no == 3, -exp_ref[...], centers)
    columns = jnp.transpose(table)
    for c in range(4):
        cen[c] = jnp.broadcast_to(columns[:, c : c + 1], (NF, BLK))


def read_lists(grid_ref, lists_f, lists_ref):
    pltpu.sync_copy(grid_ref.at[:, PTS:PACK], lists_f)
    for b in range(SLOTS):
        for j in range(NBLK):
            lists_ref[b * 4 + j] = lists_f[b * 4, j].astype(jnp.int32)


def active_list(lists_ref, own, order):
    def visit(b, n):
        named = lists_ref[b * 4] == own
        for j in range(1, NBLK):
            named = jnp.logical_or(named, lists_ref[b * 4 + j] == own)
        order[n] = b
        return n + named.astype(jnp.int32)

    return lax.fori_loop(0, SLOTS, visit, 0)


def position(lists_ref, b, own):
    at = jnp.int32(0)
    for j in range(1, NBLK):
        at = jnp.where(lists_ref[b * 4 + j] == own, j, at)
    return at


def fill_phi(lists_ref, grid_ref, b, cen, phi_hi, phi_lo):
    rows = [grid_ref[pl.ds(b * 4 + c, 1), 0:PTS] for c in range(3)]
    step = 32
    for j in range(NBLK):
        base = pl.multiple_of(lists_ref[b * 4 + j] * BLK, BLK)
        for r in range(0, BLK, step):
            at = pl.ds(base + r, step)
            center = [cen[c, at, :] for c in range(4)]
            for t in range(0, PTS, BLK):
                dx = rows[0][:, t : t + BLK] - center[0]
                dy = rows[1][:, t : t + BLK] - center[1]
                dz = rows[2][:, t : t + BLK] - center[2]
                dist = dx * dx + dy * dy + dz * dz
                hi, lo = split(jnp.exp(center[3] * dist))
                phi_hi[j * BLK + r : j * BLK + r + step, t : t + BLK] = hi
                phi_lo[j * BLK + r : j * BLK + r + step, t : t + BLK] = lo


def own_phi(at, phi_hi, phi_lo):
    where = pl.ds(pl.multiple_of(at * BLK, BLK), BLK)
    return phi_hi[where, :].astype(jnp.float32) + phi_lo[where, :].astype(jnp.float32)


def pack_kernel(points_ref, weights_ref, lists_ref, live_ref, packed_ref):
    rows = []
    for s in range(2):
        rows += [points_ref[c, s : s + 1, :] for c in range(3)] + [weights_ref[s : s + 1, :]]
    grid = jnp.concatenate(rows, axis=0)
    lane = lax.broadcasted_iota(jnp.int32, (8, PACK - PTS), 1)
    row = lax.broadcasted_iota(jnp.int32, (8, PACK - PTS), 0)
    extra = jnp.full((8, PACK - PTS), -1.0, jnp.float32)
    for s in range(2):
        for j in range(NBLK):
            named = jnp.where(s < live_ref[0], lists_ref[s, j], -1).astype(jnp.float32)
            here = jnp.logical_and(lane == j, (row >= 4) == (s == 1))
            extra = jnp.where(here, named, extra)
    for k in range(OWNERS):
        packed_ref[k, :, 0:PTS] = grid
        packed_ref[k, :, PTS:PACK] = extra


def prep_kernel(d0, d1, d2, d3, xyz_ref, atom_ref, exp_ref, cen, dens):
    piece = lax.axis_index("zl") * 2 + lax.axis_index("core")
    build_table(xyz_ref, atom_ref, exp_ref, cen)
    for i, ref in enumerate((d0, d1, d2, d3)):
        hi, lo = split(ref[...])
        at = pl.multiple_of((piece ^ i) * 32, 32)
        dens[pl.ds(at, 32), :] = hi
        dens[pl.ds(at + BLK, 32), :] = lo


def rho_kernel(grid_ref, cen, dens, rho_ref, phi_ref, lists_f, lists_ref, order):
    own = lax.axis_index("zh")
    read_lists(grid_ref, lists_f, lists_ref)
    rho_ref[...] = jnp.zeros_like(rho_ref)
    count = active_list(lists_ref, own, order)

    def visit(i, carry):
        b = order[i]
        phi_hi, phi_lo = phi_ref.at[i, 0], phi_ref.at[i, 1]
        fill_phi(lists_ref, grid_ref, b, cen, phi_hi, phi_lo)
        mixed = jnp.zeros((BLK, PTS), jnp.float32)
        for j in range(0, NBLK, 2):
            cols = [pl.ds(pl.multiple_of(lists_ref[b * 4 + j + k] * BLK, BLK), BLK) for k in range(2)]
            pair = jnp.concatenate([dens[:, cols[0]], dens[:, cols[1]]], axis=1)
            rows = slice(j * BLK, (j + 2) * BLK)
            both = dot_nn(pair, phi_hi[rows, :])
            mixed = mixed + both[:BLK] + both[BLK:] + dot_nn(pair[:BLK], phi_lo[rows, :])
        mine = own_phi(position(lists_ref, b, own), phi_hi, phi_lo)
        total = jnp.sum(mine * mixed, axis=0, keepdims=True)
        for k in range(OWNERS):
            rho_ref[k, pl.ds(b, 1), :] = total
        return carry

    lax.fori_loop(0, count, visit, 0)


def cube_root(x):
    size = jnp.abs(x)
    safe = jnp.maximum(size, 1e-37)
    y = jnp.exp(jnp.log(safe) * (1.0 / 3.0))
    y = y - (y - safe / (y * y)) * (1.0 / 3.0)
    y = jnp.where(size < 1e-37, 0.0, y)
    return jnp.where(x < 0.0, -y, y)


def matrix_kernel(grid_ref, parts_ref, phi_ref, v0, v1, v2, v3, total, root, lists_f, lists_ref, order):
    own = lax.axis_index("zh")
    piece = lax.axis_index("zl") * 2 + lax.axis_index("core")
    read_lists(grid_ref, lists_f, lists_ref)
    rho = parts_ref[0]
    for k in range(1, OWNERS):
        rho = rho + parts_ref[k]
    root[...] = cube_root(rho) * (-slater_coef)
    total[...] = jnp.zeros_like(total)
    count = active_list(lists_ref, own, order)

    def visit(i, carry):
        b = order[i]
        phi_hi, phi_lo = phi_ref.at[i, 0], phi_ref.at[i, 1]
        factor = grid_ref[pl.ds(b * 4 + 3, 1), 0:PTS] * root[pl.ds(b, 1), :]
        mine = own_phi(position(lists_ref, b, own), phi_hi, phi_lo)
        hi, lo = split(mine * factor)
        pair = jnp.concatenate([hi, lo], axis=0)
        both = dot_nt(pair, phi_hi[...])
        result = both[:BLK] + both[BLK:] + dot_nt(hi, phi_lo[...])
        for j in range(NBLK):
            cols = pl.ds(pl.multiple_of(lists_ref[b * 4 + j] * BLK, BLK), BLK)
            total[:, cols] += result[:, j * BLK : (j + 1) * BLK]
        return carry

    lax.fori_loop(0, count, visit, 0)
    for i, ref in enumerate((v0, v1, v2, v3)):
        at = pl.multiple_of((piece ^ i) * 32, 32)
        ref[...] = total[pl.ds(at, 32), :]


smem = pl.BlockSpec(memory_space=pltpu.SMEM)
vmem = pl.BlockSpec(memory_space=pltpu.VMEM)


def params(mib):
    return pltpu.CompilerParams(vmem_limit_bytes=mib << 20)


def held(x):
    return pltpu.with_memory_space_constraint(x, pltpu.VMEM)


def left(x):
    return pltpu.with_memory_space_constraint(x, pltpu.HBM)


def body(density, atom_xyz, atom_of, exponent, points, weights, lists, live):
    own_rows = density[0]
    packed = pl.pallas_call(
        pack_kernel,
        out_shape=pltpu.VMEM((OWNERS, 8, PACK), jnp.float32),
        in_specs=[vmem, vmem, smem, smem],
        out_specs=vmem,
        compiler_params=params(2),
        name="pack",
    )(left(jnp.transpose(points, (1, 0, 2))), left(weights), lists, live)
    gathered = lax.all_to_all(packed, "zh", 0, 0).reshape(SLOTS * 4, PACK)
    others = (
        lax.ppermute(own_rows, "core", SWAP),
        lax.ppermute(own_rows, "zl", SWAP),
        lax.ppermute(own_rows, ("zl", "core"), FLIP),
    )
    cen, dens = pl.pallas_call(
        prep_kernel,
        out_shape=[pltpu.VMEM((4, NF, BLK), jnp.float32), pltpu.VMEM((2 * BLK, NF), jnp.bfloat16)],
        in_specs=[vmem] * 7,
        out_specs=[vmem] * 2,
        compiler_params=params(8),
        name="prep",
    )(left(own_rows), *(held(x) for x in others), left(atom_xyz[0]), left(atom_of), left(exponent))
    lists_scratch = [
        pltpu.SMEM((SLOTS * 4, PACK - PTS), jnp.float32),
        pltpu.SMEM((SLOTS * NBLK,), jnp.int32),
        pltpu.SMEM((SLOTS + 1,), jnp.int32),
    ]
    rho, phi = pl.pallas_call(
        rho_kernel,
        out_shape=[
            pltpu.VMEM((OWNERS, SLOTS, PTS), jnp.float32),
            pltpu.VMEM((SLOTS, 2, PTS, PTS), jnp.bfloat16),
        ],
        in_specs=[vmem] * 3,
        out_specs=[vmem] * 2,
        scratch_shapes=lists_scratch,
        compiler_params=params(4),
        name="rho",
    )(held(gathered), held(cen), held(dens))
    parts = lax.all_to_all(rho, "zh", 0, 0)
    pieces = pl.pallas_call(
        matrix_kernel,
        out_shape=[pltpu.VMEM((32, NF), jnp.float32)] * 4,
        in_specs=[vmem] * 3,
        out_specs=[vmem] * 4,
        scratch_shapes=[
            pltpu.VMEM((BLK, NF), jnp.float32),
            pltpu.VMEM((SLOTS, PTS), jnp.float32),
        ]
        + lists_scratch,
        compiler_params=params(4),
        name="matrix",
    )(held(gathered), held(parts), held(phi))
    total = (
        pieces[0]
        + lax.ppermute(pieces[1], "core", SWAP)
        + lax.ppermute(pieces[2], "zl", SWAP)
        + lax.ppermute(pieces[3], ("zl", "core"), FLIP)
    )
    return total[None]


def solution(mesh):
    torus = Mesh(mesh.devices.reshape(mesh.shape["region"], OWNERS, 2, 2), ALL)
    return jax.shard_map(
        body,
        mesh=torus,
        in_specs=(
            P("region", TILE, None),
            P("region", None, None),
            P("region", None),
            P("region", None),
            P(ALL, None, None),
            P(ALL, None),
            P(ALL, None),
            P(ALL),
        ),
        out_specs=P("region", TILE, None),
        check_vma=False,
    )
```

```python
import math

import jax
import jax.numpy as jnp
from jax import lax
from jax.experimental import pallas as pl
from jax.experimental.pallas import tpu as pltpu
from jax.sharding import Mesh
from jax.sharding import PartitionSpec as P

BLK = 128
NBLK = 4
PTS = 512
NF = 1024
OWNERS = 8
SLOTS = 16
PACK = 640
FEAT = 128
MID = 1.5
TILE = ("zh", "zl", "core")
ALL = ("region", "zh", "zl", "core")
SWAP = [(0, 1), (1, 0)]

slater_coef = (3.0 / math.pi) ** (1.0 / 3.0)


def split(x):
    hi = x.astype(jnp.bfloat16)
    lo = (x - hi.astype(jnp.float32)).astype(jnp.bfloat16)
    return hi, lo


def dot_nn(a, b):
    return lax.dot_general(a, b, (((1,), (0,)), ((), ())), preferred_element_type=jnp.float32)


def dot_nt(a, b):
    return lax.dot_general(a, b, (((1,), (1,)), ((), ())), preferred_element_type=jnp.float32)


def split3(x):
    first = x.astype(jnp.bfloat16).astype(jnp.float32)
    rest = x - first
    second = rest.astype(jnp.bfloat16).astype(jnp.float32)
    return first, second, rest - second


def read_lists(grid_ref, lists_f, lists_ref):
    pltpu.sync_copy(grid_ref.at[:, PTS:PACK], lists_f)
    for b in range(SLOTS):
        for j in range(NBLK):
            lists_ref[b * 4 + j] = lists_f[b * 4, j].astype(jnp.int32)


def active_list(lists_ref, own, order):
    def visit(b, n):
        named = lists_ref[b * 4] == own
        for j in range(1, NBLK):
            named = jnp.logical_or(named, lists_ref[b * 4 + j] == own)
        order[n] = b
        return n + named.astype(jnp.int32)

    return lax.fori_loop(0, SLOTS, visit, 0)


def position(lists_ref, b, own):
    at = jnp.int32(0)
    for j in range(1, NBLK):
        at = jnp.where(lists_ref[b * 4 + j] == own, j, at)
    return at


def fill_phi(lists_ref, b, func_ref, feat, phi_hi, phi_lo):
    here = feat[b // 2]
    for j in range(NBLK):
        base = pl.multiple_of(lists_ref[b * 4 + j] * BLK, BLK)
        power = dot_nn(func_ref[b % 2, pl.ds(base, BLK), :], here)
        hi, lo = split(jnp.exp(power))
        phi_hi[j * BLK : (j + 1) * BLK, :] = hi
        phi_lo[j * BLK : (j + 1) * BLK, :] = lo


def own_phi(at, phi_hi, phi_lo):
    where = pl.ds(pl.multiple_of(at * BLK, BLK), BLK)
    return phi_hi[where, :].astype(jnp.float32) + phi_lo[where, :].astype(jnp.float32)


def pack_kernel(points_ref, weights_ref, lists_ref, live_ref, packed_ref):
    rows = []
    for s in range(2):
        rows += [points_ref[c, s : s + 1, :] for c in range(3)] + [weights_ref[s : s + 1, :]]
    grid = jnp.concatenate(rows, axis=0)
    blocks = jnp.concatenate([jnp.broadcast_to(lists_ref[s : s + 1, :], (4, NBLK)) for s in range(2)], axis=0)
    slot = lax.broadcasted_iota(jnp.int32, (8, NBLK), 0) // 4
    named = jnp.where(slot < live_ref[...], blocks, -1).astype(jnp.float32)
    for k in range(OWNERS):
        packed_ref[k, :, 0:PTS] = grid
        packed_ref[k, :, PTS:PACK] = jnp.full((8, PACK - PTS), -1.0, jnp.float32)
        packed_ref[k, :, PTS : PTS + NBLK] = named


def prep_kernel(xyz_ref, atom_ref, exp_ref, func_ref):
    atoms = lax.broadcasted_iota(jnp.int32, (256, NF), 0)
    picked = jnp.where(atoms == atom_ref[...], 1.0, 0.0).astype(jnp.bfloat16)
    parts = split3(jnp.concatenate([xyz_ref[c] for c in range(3)], axis=0) - MID)
    rows = jnp.concatenate([*parts, jnp.zeros((7, 256), jnp.float32)], axis=0)
    found = dot_nn(rows.astype(jnp.bfloat16), picked)
    x, y, z = (found[c : c + 1] + found[c + 3 : c + 4] + found[c + 6 : c + 7] for c in range(3))
    rate = exp_ref[...]
    twice = 2.0 * rate
    s1, s2, s3 = split3(jnp.concatenate([twice * x, twice * y, twice * z, -rate], axis=0))
    c1, c2, c3 = split3(-rate * (x * x + y * y + z * z))
    blank = jnp.zeros((4, NF), jnp.float32)
    side = []
    for part in (s1, s1, s2, s2, s1, s3):
        side += [part, blank]
    side += [c1, c2, c3, jnp.zeros((FEAT - 51, NF), jnp.float32)]
    columns = jnp.transpose(jnp.concatenate(side, axis=0))
    func_ref[0] = columns.astype(jnp.bfloat16)
    func_ref[1] = pltpu.roll(columns, 4, 1).astype(jnp.bfloat16)


def build_features(grid_ref, feat):
    centered = grid_ref[:, 0:PTS] - MID
    square = centered * centered
    norm = pltpu.roll(square, 1, 0) + pltpu.roll(square, 2, 0) + pltpu.roll(square, 3, 0)
    row = lax.broadcasted_iota(jnp.int32, (SLOTS * 4, PTS), 0)
    w1, w2, w3 = split3(jnp.where((row & 3) == 3, norm, centered))
    ones = jnp.ones((8, PTS), jnp.float32)
    rest = jnp.zeros((FEAT - 64, PTS), jnp.bfloat16)
    for t in range(SLOTS // 2):
        at = slice(8 * t, 8 * t + 8)
        side = [part[at] for part in (w1, w2, w1, w2, w3, w1)] + [ones, ones]
        feat[t, 0:64, :] = jnp.concatenate(side, axis=0).astype(jnp.bfloat16)
        feat[t, 64:FEAT, :] = rest


def rho_kernel(grid_ref, func_ref, d0, d1, d2, d3, rho_ref, phi_ref, dens, feat, lists_f, lists_ref, order):
    own = lax.axis_index("zh")
    piece = lax.axis_index("zl") * 2 + lax.axis_index("core")
    read_lists(grid_ref, lists_f, lists_ref)
    build_features(grid_ref, feat)
    for i, ref in enumerate((d0, d1, d2, d3)):
        hi, lo = split(ref[...])
        at = pl.multiple_of((piece ^ i) * 32, 32)
        dens[pl.ds(at, 32), :] = hi
        dens[pl.ds(at + BLK, 32), :] = lo
    rho_ref[...] = jnp.zeros_like(rho_ref)
    count = active_list(lists_ref, own, order)

    def visit(i, carry):
        b = order[i]
        phi_hi, phi_lo = phi_ref.at[i, 0], phi_ref.at[i, 1]
        fill_phi(lists_ref, b, func_ref, feat, phi_hi, phi_lo)
        mixed = jnp.zeros((BLK, PTS), jnp.float32)
        for j in range(0, NBLK, 2):
            cols = [pl.ds(pl.multiple_of(lists_ref[b * 4 + j + k] * BLK, BLK), BLK) for k in range(2)]
            pair = jnp.concatenate([dens[:, cols[0]], dens[:, cols[1]]], axis=1)
            rows = slice(j * BLK, (j + 2) * BLK)
            both = dot_nn(pair, phi_hi[rows, :])
            mixed = mixed + both[:BLK] + both[BLK:] + dot_nn(pair[:BLK], phi_lo[rows, :])
        mine = own_phi(position(lists_ref, b, own), phi_hi, phi_lo)
        total = jnp.sum(mine * mixed, axis=0, keepdims=True)
        for k in range(OWNERS):
            rho_ref[k, pl.ds(b, 1), :] = total
        return carry

    lax.fori_loop(0, count, visit, 0)


def cube_root(x):
    size = jnp.abs(x)
    safe = jnp.maximum(size, 1e-37)
    y = jnp.exp(jnp.log(safe) * (1.0 / 3.0))
    y = y - (y - safe / (y * y)) * (1.0 / 3.0)
    y = jnp.where(size < 1e-37, 0.0, y)
    return jnp.where(x < 0.0, -y, y)


def matrix_kernel(grid_ref, parts_ref, phi_ref, keep_ref, send_ref, total, root, lists_f, lists_ref, order):
    own = lax.axis_index("zh")
    piece = lax.axis_index("zl") * 2 + lax.axis_index("core")
    read_lists(grid_ref, lists_f, lists_ref)
    rho = parts_ref[0]
    for k in range(1, OWNERS):
        rho = rho + parts_ref[k]
    root[...] = cube_root(rho) * (-slater_coef)
    total[...] = jnp.zeros_like(total)
    count = active_list(lists_ref, own, order)

    def visit(i, carry):
        b = order[i]
        phi_hi, phi_lo = phi_ref.at[i, 0], phi_ref.at[i, 1]
        factor = grid_ref[pl.ds(b * 4 + 3, 1), 0:PTS] * root[pl.ds(b, 1), :]
        mine = own_phi(position(lists_ref, b, own), phi_hi, phi_lo)
        hi, lo = split(mine * factor)
        pair = jnp.concatenate([hi, lo], axis=0)
        both = dot_nt(pair, phi_hi[...])
        result = both[:BLK] + both[BLK:] + dot_nt(hi, phi_lo[...])
        for j in range(NBLK):
            cols = pl.ds(pl.multiple_of(lists_ref[b * 4 + j] * BLK, BLK), BLK)
            total[:, cols] += result[:, j * BLK : (j + 1) * BLK]
        return carry

    lax.fori_loop(0, count, visit, 0)
    for i in range(4):
        at = pl.multiple_of((piece ^ i) * 32, 32)
        (keep_ref, send_ref)[i % 2][i // 2] = total[pl.ds(at, 32), :]


vmem = pl.BlockSpec(memory_space=pltpu.VMEM)


def params(mib):
    return pltpu.CompilerParams(vmem_limit_bytes=mib << 20)


def held(x):
    return pltpu.with_memory_space_constraint(x, pltpu.VMEM)


def left(x):
    return pltpu.with_memory_space_constraint(x, pltpu.HBM)


def body(density, atom_xyz, atom_of, exponent, points, weights, lists, live):
    own_rows = density[0]
    packed = pl.pallas_call(
        pack_kernel,
        out_shape=pltpu.VMEM((OWNERS, 8, PACK), jnp.float32),
        in_specs=[vmem] * 4,
        out_specs=vmem,
        compiler_params=params(2),
        name="pack",
    )(left(jnp.transpose(points, (1, 0, 2))), left(weights), left(lists), live.reshape(1, 1))
    gathered = lax.all_to_all(packed, "zh", 0, 0).reshape(SLOTS * 4, PACK)
    far = lax.ppermute(own_rows, "zl", SWAP)
    near = lax.ppermute(own_rows, "core", SWAP)
    func = pl.pallas_call(
        prep_kernel,
        out_shape=pltpu.VMEM((2, NF, FEAT), jnp.bfloat16),
        in_specs=[vmem] * 3,
        out_specs=vmem,
        compiler_params=params(8),
        cost_estimate=pl.CostEstimate(flops=4_000_000_000, bytes_accessed=1_000_000, transcendentals=0),
        name="prep",
    )(left(jnp.transpose(atom_xyz, (1, 0, 2))), left(atom_of), left(exponent))
    far, func = lax.optimization_barrier((far, func))
    cross = lax.ppermute(far, "core", SWAP)
    lists_scratch = [
        pltpu.SMEM((SLOTS * 4, PACK - PTS), jnp.float32),
        pltpu.SMEM((SLOTS * NBLK,), jnp.int32),
        pltpu.SMEM((SLOTS + 1,), jnp.int32),
    ]
    rho, phi = pl.pallas_call(
        rho_kernel,
        out_shape=[
            pltpu.VMEM((OWNERS, SLOTS, PTS), jnp.float32),
            pltpu.VMEM((SLOTS, 2, PTS, PTS), jnp.bfloat16),
        ],
        in_specs=[vmem] * 6,
        out_specs=[vmem] * 2,
        scratch_shapes=[
            pltpu.VMEM((2 * BLK, NF), jnp.bfloat16),
            pltpu.VMEM((SLOTS // 2, FEAT, PTS), jnp.bfloat16),
        ]
        + lists_scratch,
        compiler_params=params(6),
        name="rho",
    )(held(gathered), held(func), left(own_rows), held(near), held(far), held(cross))
    parts = lax.all_to_all(rho, "zh", 0, 0)
    keep, send = pl.pallas_call(
        matrix_kernel,
        out_shape=[pltpu.VMEM((2, 32, NF), jnp.float32)] * 2,
        in_specs=[vmem] * 3,
        out_specs=[vmem] * 2,
        scratch_shapes=[
            pltpu.VMEM((BLK, NF), jnp.float32),
            pltpu.VMEM((SLOTS, PTS), jnp.float32),
        ]
        + lists_scratch,
        compiler_params=params(4),
        name="matrix",
    )(held(gathered), held(parts), held(phi))
    got = lax.ppermute(send, "core", SWAP)
    other = lax.ppermute(keep[1] + got[1], "zl", SWAP)
    return (keep[0] + got[0] + other)[None]


def solution(mesh):
    torus = Mesh(mesh.devices.reshape(mesh.shape["region"], OWNERS, 2, 2), ALL)
    return jax.shard_map(
        body,
        mesh=torus,
        in_specs=(
            P("region", TILE, None),
            P("region", None, None),
            P("region", None),
            P("region", None),
            P(ALL, None, None),
            P(ALL, None),
            P(ALL, None),
            P(ALL),
        ),
        out_specs=P("region", TILE, None),
        check_vma=False,
    )
```

```python
import math

import jax
import jax.numpy as jnp
from jax import lax
from jax.experimental import pallas as pl
from jax.experimental.pallas import tpu as pltpu
from jax.sharding import Mesh
from jax.sharding import PartitionSpec as P

BLK = 128
NBLK = 4
PTS = 512
NF = 1024
OWNERS = 8
SLOTS = 16
PACK = 640
FEAT = 128
MID = 1.5
TILE = ("zh", "zl", "core")
ALL = ("region", "zh", "zl", "core")
SWAP = [(0, 1), (1, 0)]

slater_coef = (3.0 / math.pi) ** (1.0 / 3.0)


def split(x):
    hi = x.astype(jnp.bfloat16)
    lo = (x - hi.astype(jnp.float32)).astype(jnp.bfloat16)
    return hi, lo


def dot_nn(a, b):
    return lax.dot_general(a, b, (((1,), (0,)), ((), ())), preferred_element_type=jnp.float32)


def dot_nt(a, b):
    return lax.dot_general(a, b, (((1,), (1,)), ((), ())), preferred_element_type=jnp.float32)


def split3(x):
    first = x.astype(jnp.bfloat16).astype(jnp.float32)
    rest = x - first
    second = rest.astype(jnp.bfloat16).astype(jnp.float32)
    return first, second, rest - second


def list_copies(grid_ref, lists_f, sems):
    return [
        pltpu.make_async_copy(grid_ref.at[8 * k : 8 * k + 1, PTS:PACK], lists_f.at[k : k + 1], sems.at[k])
        for k in range(OWNERS)
    ]


def block_of(lists_f, b, j):
    return lists_f[b // 2, (b % 2) * NBLK + j].astype(jnp.int32)


def columns_of(lists_f, b, j):
    return pl.ds(pl.multiple_of(block_of(lists_f, b, j) * BLK, BLK), BLK)


def active_list(lists_f, own, order):
    own = own.astype(jnp.float32)
    n = jnp.int32(0)
    last = jnp.int32(0)
    for b in range(SLOTS):
        named = lists_f[b // 2, (b % 2) * NBLK] == own
        for j in range(1, NBLK):
            named = jnp.logical_or(named, lists_f[b // 2, (b % 2) * NBLK + j] == own)
        order[n] = jnp.int32(b)
        last = jnp.where(named, b, last)
        n = n + named.astype(jnp.int32)
    order[n] = last
    return n


def position(lists_f, b, own):
    own = own.astype(jnp.float32)
    at = jnp.int32(0)
    for j in range(1, NBLK):
        at = jnp.where(lists_f[b // 2, (b % 2) * NBLK + j] == own, j, at)
    return at


def fill_phi(lists_f, b, func_ref, feat, phi_hi, phi_lo):
    here = feat[b // 2]
    for j in range(NBLK):
        power = dot_nn(func_ref[b % 2, columns_of(lists_f, b, j), :], here)
        hi, lo = split(jnp.exp(power))
        phi_hi[j * BLK : (j + 1) * BLK, :] = hi
        phi_lo[j * BLK : (j + 1) * BLK, :] = lo


def own_phi(at, phi_hi, phi_lo):
    where = pl.ds(pl.multiple_of(at * BLK, BLK), BLK)
    return phi_hi[where, :].astype(jnp.float32) + phi_lo[where, :].astype(jnp.float32)


def pack_kernel(points_any, weights_any, lists_any, live_any, packed_ref, points_ref, weights_ref, lists_ref, live_ref, sems):
    pairs = ((points_any, points_ref), (weights_any, weights_ref), (lists_any, lists_ref), (live_any, live_ref))
    copies = [pltpu.make_async_copy(pair[0], pair[1], sems.at[i]) for i, pair in enumerate(pairs)]
    for copy in copies:
        copy.start()
    for copy in copies:
        copy.wait()
    rows = []
    for s in range(2):
        rows += [points_ref[c, s : s + 1, :] for c in range(3)] + [weights_ref[s : s + 1, :]]
    grid = jnp.concatenate(rows, axis=0)
    count = live_ref[0]
    lane = lax.broadcasted_iota(jnp.int32, (8, PACK - PTS), 1)
    extra = jnp.full((8, PACK - PTS), -1.0, jnp.float32)
    for s in range(2):
        for j in range(NBLK):
            named = jnp.where(s < count, lists_ref[s, j], -1).astype(jnp.float32)
            extra = jnp.where(lane == s * NBLK + j, named, extra)
    for k in range(OWNERS):
        packed_ref[k, :, 0:PTS] = grid
        packed_ref[k, :, PTS:PACK] = extra


def prep_kernel(xyz_ref, atom_ref, exp_ref, func_ref):
    atoms = lax.broadcasted_iota(jnp.int32, (256, NF), 0)
    picked = jnp.where(atoms == atom_ref[...], 1.0, 0.0).astype(jnp.bfloat16)
    parts = split3(jnp.concatenate([xyz_ref[c] for c in range(3)], axis=0) - MID)
    rows = jnp.concatenate([*parts, jnp.zeros((7, 256), jnp.float32)], axis=0)
    found = dot_nn(rows.astype(jnp.bfloat16), picked)
    x, y, z = (found[c : c + 1] + found[c + 3 : c + 4] + found[c + 6 : c + 7] for c in range(3))
    rate = exp_ref[...]
    twice = 2.0 * rate
    s1, s2, s3 = split3(jnp.concatenate([twice * x, twice * y, twice * z, -rate], axis=0))
    c1, c2, c3 = split3(-rate * (x * x + y * y + z * z))
    blank = jnp.zeros((4, NF), jnp.float32)
    side = []
    for part in (s1, s1, s2, s2, s1, s3):
        side += [part, blank]
    side += [c1, c2, c3, jnp.zeros((FEAT - 51, NF), jnp.float32)]
    columns = jnp.transpose(jnp.concatenate(side, axis=0))
    func_ref[0] = columns.astype(jnp.bfloat16)
    func_ref[1] = pltpu.roll(columns, 4, 1).astype(jnp.bfloat16)


def build_features(grid_ref, feat):
    centered = grid_ref[:, 0:PTS] - MID
    square = centered * centered
    norm = pltpu.roll(square, 1, 0) + pltpu.roll(square, 2, 0) + pltpu.roll(square, 3, 0)
    row = lax.broadcasted_iota(jnp.int32, (SLOTS * 4, PTS), 0)
    w1, w2, w3 = split3(jnp.where((row & 3) == 3, norm, centered))
    ones = jnp.ones((8, PTS), jnp.float32)
    rest = jnp.zeros((FEAT - 64, PTS), jnp.bfloat16)
    for t in range(SLOTS // 2):
        at = slice(8 * t, 8 * t + 8)
        side = [part[at] for part in (w1, w2, w1, w2, w3, w1)] + [ones, ones]
        feat[t, 0:64, :] = jnp.concatenate(side, axis=0).astype(jnp.bfloat16)
        feat[t, 64:FEAT, :] = rest


def rho_kernel(
    grid_ref, func_ref, d0, d1, d2, d3, rho_ref, even_ref, odd_ref, dens, feat, lists_f, order, sems
):
    own = lax.axis_index("zh")
    piece = lax.axis_index("zl") * 2 + lax.axis_index("core")
    copies = list_copies(grid_ref, lists_f, sems)
    for copy in copies:
        copy.start()
    build_features(grid_ref, feat)
    for i, ref in enumerate((d0, d1, d2, d3)):
        hi, lo = split(ref[...])
        at = pl.multiple_of((piece ^ i) * 32, 32)
        dens[pl.ds(at, 32), :] = hi
        dens[pl.ds(at + BLK, 32), :] = lo
    rho_ref[...] = jnp.zeros_like(rho_ref)
    for copy in copies:
        copy.wait()
    count = active_list(lists_f, own, order)

    def make_phi(i, m, ref):
        fill_phi(lists_f, order[i], func_ref, feat, ref.at[m, 0], ref.at[m, 1])

    def make_rho(i, m, ref):
        b = order[i]
        phi_hi, phi_lo = ref.at[m, 0], ref.at[m, 1]
        mixed = jnp.zeros((BLK, PTS), jnp.float32)
        for j in range(0, NBLK, 2):
            pair = jnp.concatenate([dens[:, columns_of(lists_f, b, j + k)] for k in range(2)], axis=1)
            rows = slice(j * BLK, (j + 2) * BLK)
            both = dot_nn(pair, phi_hi[rows, :])
            mixed = mixed + both[:BLK] + both[BLK:] + dot_nn(pair[:BLK], phi_lo[rows, :])
        mine = own_phi(position(lists_f, b, own), phi_hi, phi_lo)
        total = jnp.sum(mine * mixed, axis=0, keepdims=True)
        for k in range(OWNERS):
            rho_ref[k, pl.ds(b, 1), :] = total

    pairs = (count + 1) // 2

    def visit(m, carry):
        before = jnp.maximum(m - 1, 0)
        make_phi(2 * m, m, even_ref)
        make_rho(2 * before + 1, before, odd_ref)
        make_phi(2 * m + 1, m, odd_ref)
        make_rho(2 * m, m, even_ref)
        return carry

    lax.fori_loop(0, pairs, visit, 0)

    @pl.when(pairs > 0)
    def _():
        make_rho(2 * pairs - 1, pairs - 1, odd_ref)


def cube_root(x):
    size = jnp.abs(x)
    safe = jnp.maximum(size, 1e-37)
    y = jnp.exp(jnp.log(safe) * (1.0 / 3.0))
    y = y - (y - safe / (y * y)) * (1.0 / 3.0)
    y = jnp.where(size < 1e-37, 0.0, y)
    return jnp.where(x < 0.0, -y, y)


def matrix_kernel(grid_ref, parts_ref, even_ref, odd_ref, keep_ref, send_ref, total, root, lists_f, order, sems):
    own = lax.axis_index("zh")
    piece = lax.axis_index("zl") * 2 + lax.axis_index("core")
    copies = list_copies(grid_ref, lists_f, sems)
    for copy in copies:
        copy.start()
    rho = parts_ref[0]
    for k in range(1, OWNERS):
        rho = rho + parts_ref[k]
    root[...] = cube_root(rho) * (-slater_coef)
    total[...] = jnp.zeros_like(total)
    for copy in copies:
        copy.wait()
    count = active_list(lists_f, own, order)

    def product(i, m, ref):
        b = order[i]
        phi_hi, phi_lo = ref.at[m, 0], ref.at[m, 1]
        factor = grid_ref[pl.ds(b * 4 + 3, 1), 0:PTS] * root[pl.ds(b, 1), :]
        factor = jnp.where(i < count, factor, 0.0)
        mine = own_phi(position(lists_f, b, own), phi_hi, phi_lo)
        hi, lo = split(mine * factor)
        pair = jnp.concatenate([hi, lo], axis=0)
        both = dot_nt(pair, phi_hi[...])
        return b, both[:BLK] + both[BLK:] + dot_nt(hi, phi_lo[...])

    def visit(m, carry):
        for b, result in (product(2 * m, m, even_ref), product(2 * m + 1, m, odd_ref)):
            for j in range(NBLK):
                total[:, columns_of(lists_f, b, j)] += result[:, j * BLK : (j + 1) * BLK]
        return carry

    lax.fori_loop(0, (count + 1) // 2, visit, 0)
    for i in range(4):
        at = pl.multiple_of((piece ^ i) * 32, 32)
        (keep_ref, send_ref)[i % 2][i // 2] = total[pl.ds(at, 32), :]


vmem = pl.BlockSpec(memory_space=pltpu.VMEM)


def params(mib):
    return pltpu.CompilerParams(vmem_limit_bytes=mib << 20)


def held(x):
    return pltpu.with_memory_space_constraint(x, pltpu.VMEM)


def left(x):
    return pltpu.with_memory_space_constraint(x, pltpu.HBM)


def body(density, atom_xyz, atom_of, exponent, points, weights, lists, live):
    own_rows = density[0]
    packed = pl.pallas_call(
        pack_kernel,
        out_shape=pltpu.VMEM((OWNERS, 8, PACK), jnp.float32),
        in_specs=[pl.BlockSpec(memory_space=pl.ANY)] * 4,
        out_specs=vmem,
        scratch_shapes=[
            pltpu.VMEM((3, 2, PTS), jnp.float32),
            pltpu.VMEM((2, PTS), jnp.float32),
            pltpu.SMEM((2, NBLK), jnp.int32),
            pltpu.SMEM((1,), jnp.int32),
            pltpu.SemaphoreType.DMA((4,)),
        ],
        compiler_params=params(2),
        name="pack",
    )(left(jnp.transpose(points, (1, 0, 2))), left(weights), left(lists), live)
    gathered = lax.all_to_all(packed, "zh", 0, 0).reshape(SLOTS * 4, PACK)
    far = lax.ppermute(own_rows, "zl", SWAP)
    near = lax.ppermute(own_rows, "core", SWAP)
    func = pl.pallas_call(
        prep_kernel,
        out_shape=pltpu.VMEM((2, NF, FEAT), jnp.bfloat16),
        in_specs=[vmem] * 3,
        out_specs=vmem,
        compiler_params=params(8),
        cost_estimate=pl.CostEstimate(flops=4_000_000_000, bytes_accessed=1_000_000, transcendentals=0),
        name="prep",
    )(left(jnp.transpose(atom_xyz, (1, 0, 2))), left(atom_of), left(exponent))
    far, func = lax.optimization_barrier((far, func))
    cross = lax.ppermute(far, "core", SWAP)
    lists_scratch = [
        pltpu.SMEM((OWNERS, PACK - PTS), jnp.float32),
        pltpu.SMEM((SLOTS + 1,), jnp.int32),
        pltpu.SemaphoreType.DMA((OWNERS,)),
    ]
    rho, even, odd = pl.pallas_call(
        rho_kernel,
        out_shape=[
            pltpu.VMEM((OWNERS, SLOTS, PTS), jnp.float32),
            pltpu.VMEM((SLOTS // 2, 2, PTS, PTS), jnp.bfloat16),
            pltpu.VMEM((SLOTS // 2, 2, PTS, PTS), jnp.bfloat16),
        ],
        in_specs=[vmem] * 6,
        out_specs=[vmem] * 3,
        scratch_shapes=[
            pltpu.VMEM((2 * BLK, NF), jnp.bfloat16),
            pltpu.VMEM((SLOTS // 2, FEAT, PTS), jnp.bfloat16),
        ]
        + lists_scratch,
        compiler_params=params(6),
        name="rho",
    )(held(gathered), held(func), held(own_rows), held(near), held(far), held(cross))
    parts = lax.all_to_all(rho, "zh", 0, 0)
    keep, send = pl.pallas_call(
        matrix_kernel,
        out_shape=[pltpu.VMEM((2, 32, NF), jnp.float32)] * 2,
        in_specs=[vmem] * 4,
        out_specs=[vmem] * 2,
        scratch_shapes=[
            pltpu.VMEM((BLK, NF), jnp.float32),
            pltpu.VMEM((SLOTS, PTS), jnp.float32),
        ]
        + lists_scratch,
        compiler_params=params(4),
        name="matrix",
    )(held(gathered), held(parts), held(even), held(odd))
    got = lax.ppermute(send, "core", SWAP)
    other = lax.ppermute(keep[1] + got[1], "zl", SWAP)
    return (keep[0] + got[0] + other)[None]


def solution(mesh):
    torus = Mesh(mesh.devices.reshape(mesh.shape["region"], OWNERS, 2, 2), ALL)
    return jax.shard_map(
        body,
        mesh=torus,
        in_specs=(
            P("region", TILE, None),
            P("region", None, None),
            P("region", None),
            P("region", None),
            P(ALL, None, None),
            P(ALL, None),
            P(ALL, None),
            P(ALL),
        ),
        out_specs=P("region", TILE, None),
        check_vma=False,
    )
```

```python
import math

import jax
import jax.numpy as jnp
from jax import lax
from jax.experimental import pallas as pl
from jax.experimental.pallas import tpu as pltpu
from jax.sharding import Mesh
from jax.sharding import PartitionSpec as P

BLK = 128
NBLK = 4
PTS = 512
NF = 1024
OWNERS = 8
SLOTS = 16
PACK = 640
FEAT = 64
KEPT = 10
STEP = 16
MID = 1.5
TILE = ("zh", "zl", "core")
ALL = ("region", "zh", "zl", "core")
SWAP = [(0, 1), (1, 0)]

slater_coef = (3.0 / math.pi) ** (1.0 / 3.0)


def split(x):
    hi = x.astype(jnp.bfloat16)
    lo = (x - hi.astype(jnp.float32)).astype(jnp.bfloat16)
    return hi, lo


def dot_nn(a, b):
    return lax.dot_general(a, b, (((1,), (0,)), ((), ())), preferred_element_type=jnp.float32)


def dot_nt(a, b):
    return lax.dot_general(a, b, (((1,), (1,)), ((), ())), preferred_element_type=jnp.float32)


def split3(x):
    first = x.astype(jnp.bfloat16).astype(jnp.float32)
    rest = x - first
    second = rest.astype(jnp.bfloat16).astype(jnp.float32)
    return first, second, rest - second


def list_copies(grid_ref, lists_f, sems):
    return [
        pltpu.make_async_copy(grid_ref.at[8 * k : 8 * k + 1, PTS:PACK], lists_f.at[k : k + 1], sems.at[k])
        for k in range(OWNERS)
    ]


def make_plan(lists_f, own, plan, seen):
    own_f = own.astype(jnp.float32)
    for k in range(OWNERS):
        seen[k] = 0
    n = jnp.int32(0)
    for b in range(SLOTS):
        listed = [lists_f[b // 2, (b % 2) * NBLK + j] for j in range(NBLK)]
        at = jnp.int32(0)
        named = jnp.int32(0)
        for j in range(NBLK):
            same = listed[j] == own_f
            at = jnp.where(same, j, at)
            named = jnp.where(same, 1, named)
        row = n * STEP
        plan[row] = jnp.int32(b)
        plan[row + 9] = at
        for j in range(NBLK):
            block = jnp.maximum(listed[j].astype(jnp.int32), 0)
            plan[row + 1 + j] = block
            rank = seen[block]
            plan[row + 5 + j] = rank
            seen[block] = rank + named
        n = n + named
    last = jnp.maximum(n - 1, 0) * STEP
    for k in range(10):
        plan[n * STEP + k] = plan[last + k]
    return n


def crowded(grid_ref):
    lists = jnp.concatenate([grid_ref[8 * k : 8 * k + 1, PTS:PACK] for k in range(OWNERS)], axis=0)
    lane = lax.broadcasted_iota(jnp.int32, (OWNERS, PACK - PTS), 1).astype(jnp.float32)
    most = jnp.zeros((1, PACK - PTS), jnp.float32)
    marks = []
    for s in range(2):
        mark = jnp.zeros((OWNERS, PACK - PTS), jnp.float32)
        for j in range(NBLK):
            mark = jnp.where(lists[:, s * NBLK + j : s * NBLK + j + 1] == lane, 1.0, mark)
        marks.append(mark)
    for k in range(OWNERS):
        both = sum(mark * mark[:, k : k + 1] for mark in marks)
        total = jnp.sum(both, axis=0, keepdims=True)
        most = jnp.maximum(most, jnp.where(lane[0:1] == k, 0.0, total))
    return (jnp.max(most) > KEPT).astype(jnp.int32)


def columns_of(plan, i, j):
    return pl.ds(pl.multiple_of(plan[i * STEP + 1 + j] * BLK, BLK), BLK)


def fill_phi(plan, i, func_ref, feat, phi_hi, phi_lo):
    b = plan[i * STEP]
    here = feat[b // 2]
    for j in range(NBLK):
        power = dot_nn(func_ref[b % 2, columns_of(plan, i, j), :], here)
        hi, lo = split(jnp.exp(power))
        phi_hi[j * BLK : (j + 1) * BLK, :] = hi
        phi_lo[j * BLK : (j + 1) * BLK, :] = lo


def own_phi(at, phi_hi, phi_lo):
    where = pl.ds(pl.multiple_of(at * BLK, BLK), BLK)
    return phi_hi[where, :].astype(jnp.float32) + phi_lo[where, :].astype(jnp.float32)


def pack_kernel(points_any, weights_any, lists_any, live_any, packed_ref, points_ref, weights_ref, lists_ref, live_ref, sems):
    pairs = ((points_any, points_ref), (weights_any, weights_ref), (lists_any, lists_ref), (live_any, live_ref))
    copies = [pltpu.make_async_copy(pair[0], pair[1], sems.at[i]) for i, pair in enumerate(pairs)]
    for copy in copies:
        copy.start()
    for copy in copies:
        copy.wait()
    rows = []
    for s in range(2):
        rows += [points_ref[c, s : s + 1, :] for c in range(3)] + [weights_ref[s : s + 1, :]]
    grid = jnp.concatenate(rows, axis=0)
    count = live_ref[0]
    lane = lax.broadcasted_iota(jnp.int32, (8, PACK - PTS), 1)
    extra = jnp.full((8, PACK - PTS), -1.0, jnp.float32)
    for s in range(2):
        for j in range(NBLK):
            named = jnp.where(s < count, lists_ref[s, j], -1).astype(jnp.float32)
            extra = jnp.where(lane == s * NBLK + j, named, extra)
    for k in range(OWNERS):
        packed_ref[k, :, 0:PTS] = grid
        packed_ref[k, :, PTS:PACK] = extra


def prep_kernel(xyz_ref, atom_ref, exp_ref, func_ref):
    atoms = lax.broadcasted_iota(jnp.int32, (256, NF), 0)
    picked = jnp.where(atoms == atom_ref[...], 1.0, 0.0).astype(jnp.bfloat16)
    parts = split3(jnp.concatenate([xyz_ref[c] for c in range(3)], axis=0) - MID)
    rows = jnp.concatenate([*parts, jnp.zeros((7, 256), jnp.float32)], axis=0)
    found = dot_nn(rows.astype(jnp.bfloat16), picked)
    x, y, z = (found[c : c + 1] + found[c + 3 : c + 4] + found[c + 6 : c + 7] for c in range(3))
    rate = exp_ref[...]
    twice = 2.0 * rate
    s1, s2, s3 = split3(jnp.concatenate([twice * x, twice * y, twice * z, -rate], axis=0))
    c1, c2, c3 = split3(-rate * (x * x + y * y + z * z))
    blank = jnp.zeros((4, NF), jnp.float32)
    side = []
    for part in (s1, s1, s2, s2, s1, s3):
        side += [part, blank]
    side += [c1, c2, c3, jnp.zeros((FEAT - 51, NF), jnp.float32)]
    columns = jnp.transpose(jnp.concatenate(side, axis=0))
    func_ref[0] = columns.astype(jnp.bfloat16)
    func_ref[1] = pltpu.roll(columns, 4, 1).astype(jnp.bfloat16)


def build_features(grid_ref, feat):
    centered = grid_ref[:, 0:PTS] - MID
    square = centered * centered
    norm = pltpu.roll(square, 1, 0) + pltpu.roll(square, 2, 0) + pltpu.roll(square, 3, 0)
    row = lax.broadcasted_iota(jnp.int32, (SLOTS * 4, PTS), 0)
    w1, w2, w3 = split3(jnp.where((row & 3) == 3, norm, centered))
    ones = jnp.ones((8, PTS), jnp.float32)
    for t in range(SLOTS // 2):
        at = slice(8 * t, 8 * t + 8)
        side = [part[at] for part in (w1, w2, w1, w2, w3, w1)] + [ones, ones]
        feat[t] = jnp.concatenate(side, axis=0).astype(jnp.bfloat16)


def rho_kernel(
    grid_ref, func_ref, d0, d1, d2, d3, first_ref, rest_ref, even_any, odd_any, plan, count_ref, crowd_ref,
    even_ref, odd_ref, dens, feat, rows, lists_f, seen, sems, out_sems
):
    own = lax.axis_index("zh")
    piece = lax.axis_index("zl") * 2 + lax.axis_index("core")
    copies = list_copies(grid_ref, lists_f, sems)
    for copy in copies:
        copy.start()
    build_features(grid_ref, feat)
    for copy in copies:
        copy.wait()
    crowd_ref[0] = crowded(grid_ref)
    for i, ref in enumerate((d0, d1, d2, d3)):
        hi, lo = split(ref[...])
        at = pl.multiple_of((piece ^ i) * 32, 32)
        dens[pl.ds(at, 32), :] = hi
        dens[pl.ds(at + BLK, 32), :] = lo
    rows[...] = jnp.zeros_like(rows)
    count = make_plan(lists_f, own, plan, seen)
    count_ref[0] = count

    def make_phi(i, m, ref):
        fill_phi(plan, i, func_ref, feat, ref.at[m, 0], ref.at[m, 1])

    def make_rho(i, m, ref):
        phi_hi, phi_lo = ref.at[m, 0], ref.at[m, 1]
        mixed = jnp.zeros((BLK, PTS), jnp.float32)
        for j in range(0, NBLK, 2):
            pair = jnp.concatenate([dens[:, columns_of(plan, i, j + k)] for k in range(2)], axis=1)
            part = slice(j * BLK, (j + 2) * BLK)
            both = dot_nn(pair, phi_hi[part, :])
            mixed = mixed + both[:BLK] + both[BLK:] + dot_nn(pair[:BLK], phi_lo[part, :])
        mine = own_phi(plan[i * STEP + 9], phi_hi, phi_lo)
        total = jnp.sum(mine * mixed, axis=0, keepdims=True)
        for j in range(NBLK):
            at = plan[i * STEP + 1 + j] * (SLOTS * NBLK) + plan[i * STEP + 5 + j] * NBLK
            for t in range(PTS // BLK):
                rows[pl.ds(at + t, 1), :] = total[:, t * BLK : (t + 1) * BLK]

    def stores(m):
        return (
            pltpu.make_async_copy(even_ref.at[m], even_any.at[m], out_sems.at[m, 0]),
            pltpu.make_async_copy(odd_ref.at[m], odd_any.at[m], out_sems.at[m, 1]),
        )

    pairs = (count + 1) // 2

    def visit(m, carry):
        before = jnp.maximum(m - 1, 0)
        make_phi(2 * m, m, even_ref)
        make_rho(2 * before + 1, before, odd_ref)
        make_phi(2 * m + 1, m, odd_ref)
        make_rho(2 * m, m, even_ref)
        for store in stores(m):
            store.start()
        return carry

    lax.fori_loop(0, pairs, visit, 0)

    @pl.when(pairs > 0)
    def _():
        make_rho(2 * pairs - 1, pairs - 1, odd_ref)

    for k in range(OWNERS):
        at = k * SLOTS * NBLK
        first_ref[k] = rows[at : at + KEPT * NBLK, :]
        rest_ref[k] = rows[at + KEPT * NBLK : at + SLOTS * NBLK, :]

    def finish(m, carry):
        for store in stores(m):
            store.wait()
        return carry

    lax.fori_loop(0, pairs, finish, 0)


def cube_root(x):
    size = jnp.abs(x)
    safe = jnp.maximum(size, 1e-37)
    y = jnp.exp(jnp.log(safe) * (1.0 / 3.0))
    y = y - (y - safe / (y * y)) * (1.0 / 3.0)
    y = jnp.where(size < 1e-37, 0.0, y)
    return jnp.where(x < 0.0, -y, y)


def matrix_kernel(
    grid_ref, first_ref, rest_ref, even_any, odd_any, plan, count_ref, keep_ref, send_ref,
    total, parts, root, even_ref, odd_ref, sems
):
    piece = lax.axis_index("zl") * 2 + lax.axis_index("core")
    count = count_ref[0]
    pairs = (count + 1) // 2

    def loads(m):
        at = m % 2
        return (
            pltpu.make_async_copy(even_any.at[m], even_ref.at[at], sems.at[at, 0]),
            pltpu.make_async_copy(odd_any.at[m], odd_ref.at[at], sems.at[at, 1]),
        )

    @pl.when(pairs > 0)
    def _():
        for load in loads(0):
            load.start()

    for k in range(OWNERS):
        at = k * SLOTS * NBLK
        parts[at : at + KEPT * NBLK, :] = first_ref[k]
        parts[at + KEPT * NBLK : at + SLOTS * NBLK, :] = rest_ref[k]
    root[...] = jnp.zeros_like(root)
    total[...] = jnp.zeros_like(total)

    def gather(i, carry):
        at = [plan[i * STEP + 1 + j] * (SLOTS * NBLK) + plan[i * STEP + 5 + j] * NBLK for j in range(NBLK)]
        sums = [sum(parts[pl.ds(at[j] + t, 1), :] for j in range(NBLK)) for t in range(PTS // BLK)]
        root[pl.ds(i, 1), :] = jnp.concatenate(sums, axis=1)
        return carry

    lax.fori_loop(0, count, gather, 0)
    root[...] = cube_root(root[...]) * (-slater_coef)

    def product(i, at, ref):
        phi_hi, phi_lo = ref.at[at, 0], ref.at[at, 1]
        factor = grid_ref[pl.ds(plan[i * STEP] * 4 + 3, 1), 0:PTS] * root[pl.ds(jnp.minimum(i, SLOTS - 1), 1), :]
        factor = jnp.where(i < count, factor, 0.0)
        mine = own_phi(plan[i * STEP + 9], phi_hi, phi_lo)
        hi, lo = split(mine * factor)
        pair = jnp.concatenate([hi, lo], axis=0)
        both = dot_nt(pair, phi_hi[...])
        return both[:BLK] + both[BLK:] + dot_nt(hi, phi_lo[...])

    def visit(m, carry):
        @pl.when(m + 1 < pairs)
        def _():
            for load in loads(m + 1):
                load.start()

        for load in loads(m):
            load.wait()
        results = product(2 * m, m % 2, even_ref), product(2 * m + 1, m % 2, odd_ref)
        for k in range(2):
            for j in range(NBLK):
                total[:, columns_of(plan, 2 * m + k, j)] += results[k][:, j * BLK : (j + 1) * BLK]
        return carry

    lax.fori_loop(0, pairs, visit, 0)
    for i in range(4):
        at = pl.multiple_of((piece ^ i) * 32, 32)
        (keep_ref, send_ref)[i % 2][i // 2] = total[pl.ds(at, 32), :]


smem = pl.BlockSpec(memory_space=pltpu.SMEM)
vmem = pl.BlockSpec(memory_space=pltpu.VMEM)


def params(mib):
    return pltpu.CompilerParams(vmem_limit_bytes=mib << 20)


def held(x):
    return pltpu.with_memory_space_constraint(x, pltpu.VMEM)


def left(x):
    return pltpu.with_memory_space_constraint(x, pltpu.HBM)


def body(density, atom_xyz, atom_of, exponent, points, weights, lists, live):
    own_rows = density[0]
    packed = pl.pallas_call(
        pack_kernel,
        out_shape=pltpu.VMEM((OWNERS, 8, PACK), jnp.float32),
        in_specs=[pl.BlockSpec(memory_space=pl.ANY)] * 4,
        out_specs=vmem,
        scratch_shapes=[
            pltpu.VMEM((3, 2, PTS), jnp.float32),
            pltpu.VMEM((2, PTS), jnp.float32),
            pltpu.SMEM((2, NBLK), jnp.int32),
            pltpu.SMEM((1,), jnp.int32),
            pltpu.SemaphoreType.DMA((4,)),
        ],
        compiler_params=params(2),
        name="pack",
    )(left(jnp.transpose(points, (1, 0, 2))), left(weights), left(lists), live)
    gathered = lax.all_to_all(packed, "zh", 0, 0).reshape(SLOTS * 4, PACK)
    far = lax.ppermute(own_rows, "zl", SWAP)
    near = lax.ppermute(own_rows, "core", SWAP)
    func = pl.pallas_call(
        prep_kernel,
        out_shape=pltpu.VMEM((2, NF, FEAT), jnp.bfloat16),
        in_specs=[vmem] * 3,
        out_specs=vmem,
        compiler_params=params(8),
        cost_estimate=pl.CostEstimate(flops=4_000_000_000, bytes_accessed=1_000_000, transcendentals=0),
        name="prep",
    )(left(jnp.transpose(atom_xyz, (1, 0, 2))), left(atom_of), left(exponent))
    far, func = lax.optimization_barrier((far, func))
    cross = lax.ppermute(far, "core", SWAP)
    first, rest, even, odd, plan, count, crowd = pl.pallas_call(
        rho_kernel,
        out_shape=[
            pltpu.VMEM((OWNERS, KEPT * NBLK, BLK), jnp.float32),
            pltpu.VMEM((OWNERS, (SLOTS - KEPT) * NBLK, BLK), jnp.float32),
            pltpu.HBM((SLOTS // 2, 2, PTS, PTS), jnp.bfloat16),
            pltpu.HBM((SLOTS // 2, 2, PTS, PTS), jnp.bfloat16),
            jax.ShapeDtypeStruct(((SLOTS + 1) * STEP,), jnp.int32),
            jax.ShapeDtypeStruct((1,), jnp.int32),
            jax.ShapeDtypeStruct((1,), jnp.int32),
        ],
        in_specs=[vmem] * 6,
        out_specs=[vmem] * 2 + [pl.BlockSpec(memory_space=pl.ANY)] * 2 + [smem] * 3,
        scratch_shapes=[
            pltpu.VMEM((SLOTS // 2, 2, PTS, PTS), jnp.bfloat16),
            pltpu.VMEM((SLOTS // 2, 2, PTS, PTS), jnp.bfloat16),
            pltpu.VMEM((2 * BLK, NF), jnp.bfloat16),
            pltpu.VMEM((SLOTS // 2, FEAT, PTS), jnp.bfloat16),
            pltpu.VMEM((OWNERS * SLOTS * NBLK, BLK), jnp.float32),
            pltpu.SMEM((OWNERS, PACK - PTS), jnp.float32),
            pltpu.SMEM((OWNERS,), jnp.int32),
            pltpu.SemaphoreType.DMA((OWNERS,)),
            pltpu.SemaphoreType.DMA((SLOTS // 2, 2)),
        ],
        compiler_params=params(24),
        name="rho",
    )(held(gathered), held(func), held(own_rows), held(near), held(far), held(cross))
    parts = lax.all_to_all(first, "zh", 0, 0)
    others = lax.cond(crowd[0] > 0, lambda x: lax.all_to_all(x, "zh", 0, 0), lambda x: x, rest)
    keep, send = pl.pallas_call(
        matrix_kernel,
        out_shape=[pltpu.VMEM((2, 32, NF), jnp.float32)] * 2,
        in_specs=[vmem] * 3 + [pl.BlockSpec(memory_space=pl.ANY)] * 2 + [smem] * 2,
        out_specs=[vmem] * 2,
        scratch_shapes=[
            pltpu.VMEM((BLK, NF), jnp.float32),
            pltpu.VMEM((OWNERS * SLOTS * NBLK, BLK), jnp.float32),
            pltpu.VMEM((SLOTS, PTS), jnp.float32),
            pltpu.VMEM((2, 2, PTS, PTS), jnp.bfloat16),
            pltpu.VMEM((2, 2, PTS, PTS), jnp.bfloat16),
            pltpu.SemaphoreType.DMA((2, 2)),
        ],
        compiler_params=params(8),
        name="matrix",
    )(held(gathered), held(parts), held(others), left(even), left(odd), plan, count)
    got = lax.ppermute(send, "core", SWAP)
    other = lax.ppermute(keep[1] + got[1], "zl", SWAP)
    return (keep[0] + got[0] + other)[None]


def solution(mesh):
    torus = Mesh(mesh.devices.reshape(mesh.shape["region"], OWNERS, 2, 2), ALL)
    return jax.shard_map(
        body,
        mesh=torus,
        in_specs=(
            P("region", TILE, None),
            P("region", None, None),
            P("region", None),
            P("region", None),
            P(ALL, None, None),
            P(ALL, None),
            P(ALL, None),
            P(ALL),
        ),
        out_specs=P("region", TILE, None),
        check_vma=False,
    )
```

```python
import functools
import math

import jax
import jax.numpy as jnp
from jax import lax
from jax.experimental import pallas as pl
from jax.experimental.pallas import tpu as pltpu
from jax.sharding import Mesh
from jax.sharding import PartitionSpec as P

BLK = 128
NBLK = 4
PTS = 512
NF = 1024
OWNERS = 8
SLOTS = 16
PACK = 640
FEAT = 64
KEPT = 10
STEP = 16
MID = 1.5
TILE = ("zh", "zl", "core")
ALL = ("region", "zh", "zl", "core")
SWAP = [(0, 1), (1, 0)]

slater_coef = (3.0 / math.pi) ** (1.0 / 3.0)


def split(x):
    hi = x.astype(jnp.bfloat16)
    lo = (x - hi.astype(jnp.float32)).astype(jnp.bfloat16)
    return hi, lo


def dot_nn(a, b):
    return lax.dot_general(a, b, (((1,), (0,)), ((), ())), preferred_element_type=jnp.float32)


def dot_nt(a, b):
    return lax.dot_general(a, b, (((1,), (1,)), ((), ())), preferred_element_type=jnp.float32)


def split3(x):
    first = x.astype(jnp.bfloat16).astype(jnp.float32)
    rest = x - first
    second = rest.astype(jnp.bfloat16).astype(jnp.float32)
    return first, second, rest - second


def list_copies(grid_ref, lists_f, sems):
    return [
        pltpu.make_async_copy(grid_ref.at[8 * k : 8 * k + 1, PTS:PACK], lists_f.at[k : k + 1], sems.at[k])
        for k in range(OWNERS)
    ]


def make_plan(lists_f, own, plan, seen):
    own_f = own.astype(jnp.float32)
    for k in range(OWNERS):
        seen[k] = 0
    n = jnp.int32(0)
    for b in range(SLOTS):
        listed = [lists_f[b // 2, (b % 2) * NBLK + j] for j in range(NBLK)]
        at = jnp.int32(0)
        named = jnp.int32(0)
        for j in range(NBLK):
            same = listed[j] == own_f
            at = jnp.where(same, j, at)
            named = jnp.where(same, 1, named)
        row = n * STEP
        plan[row] = jnp.int32(b)
        plan[row + 9] = at
        for j in range(NBLK):
            block = jnp.maximum(listed[j].astype(jnp.int32), 0)
            plan[row + 1 + j] = block
            rank = seen[block]
            plan[row + 5 + j] = rank
            seen[block] = rank + named
        n = n + named
    last = jnp.maximum(n - 1, 0) * STEP
    for k in range(10):
        plan[n * STEP + k] = plan[last + k]
    return n


def crowd_kernel(grid_ref, crowd_ref):
    lists = jnp.concatenate([grid_ref[8 * k : 8 * k + 1, PTS:PACK] for k in range(OWNERS)], axis=0)
    lane = lax.broadcasted_iota(jnp.int32, (OWNERS, PACK - PTS), 1).astype(jnp.float32)
    most = jnp.zeros((1, PACK - PTS), jnp.float32)
    marks = []
    for s in range(2):
        mark = jnp.zeros((OWNERS, PACK - PTS), jnp.float32)
        for j in range(NBLK):
            mark = jnp.where(lists[:, s * NBLK + j : s * NBLK + j + 1] == lane, 1.0, mark)
        marks.append(mark)
    for k in range(OWNERS):
        both = sum(mark * mark[:, k : k + 1] for mark in marks)
        total = jnp.sum(both, axis=0, keepdims=True)
        most = jnp.maximum(most, jnp.where(lane[0:1] == k, 0.0, total))
    crowd_ref[0] = (jnp.max(most) > KEPT).astype(jnp.int32)


def columns_of(plan, i, j):
    return pl.ds(pl.multiple_of(plan[i * STEP + 1 + j] * BLK, BLK), BLK)


def fill_phi(plan, i, func_ref, feat, phi_hi, phi_lo):
    b = plan[i * STEP]
    here = feat[b // 2]
    for j in range(NBLK):
        power = dot_nn(func_ref[b % 2, columns_of(plan, i, j), :], here)
        hi, lo = split(jnp.exp(power))
        phi_hi[j * BLK : (j + 1) * BLK, :] = hi
        phi_lo[j * BLK : (j + 1) * BLK, :] = lo


def own_phi(at, phi_hi, phi_lo):
    where = pl.ds(pl.multiple_of(at * BLK, BLK), BLK)
    return phi_hi[where, :].astype(jnp.float32) + phi_lo[where, :].astype(jnp.float32)


def pack_kernel(points_any, weights_any, lists_any, live_any, packed_ref, points_ref, weights_ref, lists_ref, live_ref, sems):
    pairs = ((points_any, points_ref), (weights_any, weights_ref), (lists_any, lists_ref), (live_any, live_ref))
    copies = [pltpu.make_async_copy(pair[0], pair[1], sems.at[i]) for i, pair in enumerate(pairs)]
    for copy in copies:
        copy.start()
    for copy in copies:
        copy.wait()
    rows = []
    for s in range(2):
        rows += [points_ref[c, s : s + 1, :] for c in range(3)] + [weights_ref[s : s + 1, :]]
    grid = jnp.concatenate(rows, axis=0)
    count = live_ref[0]
    lane = lax.broadcasted_iota(jnp.int32, (8, PACK - PTS), 1)
    extra = jnp.full((8, PACK - PTS), -1.0, jnp.float32)
    for s in range(2):
        for j in range(NBLK):
            named = jnp.where(s < count, lists_ref[s, j], -1).astype(jnp.float32)
            extra = jnp.where(lane == s * NBLK + j, named, extra)
    for k in range(OWNERS):
        packed_ref[k, :, 0:PTS] = grid
        packed_ref[k, :, PTS:PACK] = extra


def prep_kernel(xyz_ref, atom_ref, exp_ref, func_ref):
    atoms = lax.broadcasted_iota(jnp.int32, (256, NF), 0)
    picked = jnp.where(atoms == atom_ref[...], 1.0, 0.0).astype(jnp.bfloat16)
    parts = split3(jnp.concatenate([xyz_ref[c] for c in range(3)], axis=0) - MID)
    rows = jnp.concatenate([*parts, jnp.zeros((7, 256), jnp.float32)], axis=0)
    found = dot_nn(rows.astype(jnp.bfloat16), picked)
    x, y, z = (found[c : c + 1] + found[c + 3 : c + 4] + found[c + 6 : c + 7] for c in range(3))
    rate = exp_ref[...]
    twice = 2.0 * rate
    s1, s2, s3 = split3(jnp.concatenate([twice * x, twice * y, twice * z, -rate], axis=0))
    c1, c2, c3 = split3(-rate * (x * x + y * y + z * z))
    blank = jnp.zeros((4, NF), jnp.float32)
    side = []
    for part in (s1, s1, s2, s2, s1, s3):
        side += [part, blank]
    side += [c1, c2, c3, jnp.zeros((FEAT - 51, NF), jnp.float32)]
    columns = jnp.transpose(jnp.concatenate(side, axis=0))
    func_ref[0] = columns.astype(jnp.bfloat16)
    func_ref[1] = pltpu.roll(columns, 4, 1).astype(jnp.bfloat16)


def build_features(grid_ref, feat):
    centered = grid_ref[:, 0:PTS] - MID
    square = centered * centered
    norm = pltpu.roll(square, 1, 0) + pltpu.roll(square, 2, 0) + pltpu.roll(square, 3, 0)
    row = lax.broadcasted_iota(jnp.int32, (SLOTS * 4, PTS), 0)
    w1, w2, w3 = split3(jnp.where((row & 3) == 3, norm, centered))
    ones = jnp.ones((8, PTS), jnp.float32)
    for t in range(SLOTS // 2):
        at = slice(8 * t, 8 * t + 8)
        side = [part[at] for part in (w1, w2, w1, w2, w3, w1)] + [ones, ones]
        feat[t] = jnp.concatenate(side, axis=0).astype(jnp.bfloat16)


def rho_kernel(
    grid_ref, func_ref, d0, d1, d2, d3, first_ref, rest_ref, even_ref, odd_ref, plan, count_ref,
    dens, feat, rows, lists_f, seen, sems
):
    own = lax.axis_index("zh")
    piece = lax.axis_index("zl") * 2 + lax.axis_index("core")
    copies = list_copies(grid_ref, lists_f, sems)
    for copy in copies:
        copy.start()
    build_features(grid_ref, feat)
    for copy in copies:
        copy.wait()
    for i, ref in enumerate((d0, d1, d2, d3)):
        hi, lo = split(ref[...])
        at = pl.multiple_of((piece ^ i) * 32, 32)
        dens[pl.ds(at, 32), :] = hi
        dens[pl.ds(at + BLK, 32), :] = lo
    rows[...] = jnp.zeros_like(rows)
    count = make_plan(lists_f, own, plan, seen)
    count_ref[0] = count

    def make_phi(i, m, ref):
        fill_phi(plan, i, func_ref, feat, ref.at[m, 0], ref.at[m, 1])

    def make_rho(i, m, ref):
        phi_hi, phi_lo = ref.at[m, 0], ref.at[m, 1]
        mixed = jnp.zeros((BLK, PTS), jnp.float32)
        for j in range(0, NBLK, 2):
            pair = jnp.concatenate([dens[:, columns_of(plan, i, j + k)] for k in range(2)], axis=1)
            part = slice(j * BLK, (j + 2) * BLK)
            both = dot_nn(pair, phi_hi[part, :])
            mixed = mixed + both[:BLK] + both[BLK:] + dot_nn(pair[:BLK], phi_lo[part, :])
        mine = own_phi(plan[i * STEP + 9], phi_hi, phi_lo)
        total = jnp.sum(mine * mixed, axis=0, keepdims=True)
        for j in range(NBLK):
            at = plan[i * STEP + 1 + j] * (SLOTS * NBLK) + plan[i * STEP + 5 + j] * NBLK
            for t in range(PTS // BLK):
                rows[pl.ds(at + t, 1), :] = total[:, t * BLK : (t + 1) * BLK]

    pairs = (count + 1) // 2

    def visit(m, carry):
        before = jnp.maximum(m - 1, 0)
        make_phi(2 * m, m, even_ref)
        make_rho(2 * before + 1, before, odd_ref)
        make_phi(2 * m + 1, m, odd_ref)
        make_rho(2 * m, m, even_ref)
        return carry

    lax.fori_loop(0, pairs, visit, 0)

    @pl.when(pairs > 0)
    def _():
        make_rho(2 * pairs - 1, pairs - 1, odd_ref)

    for k in range(OWNERS):
        at = k * SLOTS * NBLK
        first_ref[k] = rows[at : at + KEPT * NBLK, :]
        rest_ref[k] = rows[at + KEPT * NBLK : at + SLOTS * NBLK, :]


def cube_root(x):
    size = jnp.abs(x)
    safe = jnp.maximum(size, 1e-37)
    y = jnp.exp(jnp.log(safe) * (1.0 / 3.0))
    y = y - (y - safe / (y * y)) * (1.0 / 3.0)
    y = jnp.where(size < 1e-37, 0.0, y)
    return jnp.where(x < 0.0, -y, y)


def matrix_kernel(
    grid_ref, first_ref, rest_ref, even_ref, odd_ref, plan, count_ref, keep_ref, send_ref, total, parts, root
):
    piece = lax.axis_index("zl") * 2 + lax.axis_index("core")
    count = count_ref[0]
    pairs = (count + 1) // 2

    for k in range(OWNERS):
        at = k * SLOTS * NBLK
        parts[at : at + KEPT * NBLK, :] = first_ref[k]
        parts[at + KEPT * NBLK : at + SLOTS * NBLK, :] = rest_ref[k]
    root[...] = jnp.zeros_like(root)
    total[...] = jnp.zeros_like(total)

    def gather(i, carry):
        at = [plan[i * STEP + 1 + j] * (SLOTS * NBLK) + plan[i * STEP + 5 + j] * NBLK for j in range(NBLK)]
        sums = [sum(parts[pl.ds(at[j] + t, 1), :] for j in range(NBLK)) for t in range(PTS // BLK)]
        root[pl.ds(i, 1), :] = jnp.concatenate(sums, axis=1)
        return carry

    lax.fori_loop(0, count, gather, 0)
    root[...] = cube_root(root[...]) * (-slater_coef)

    def product(i, at, ref):
        phi_hi, phi_lo = ref.at[at, 0], ref.at[at, 1]
        factor = grid_ref[pl.ds(plan[i * STEP] * 4 + 3, 1), 0:PTS] * root[pl.ds(jnp.minimum(i, SLOTS - 1), 1), :]
        factor = jnp.where(i < count, factor, 0.0)
        mine = own_phi(plan[i * STEP + 9], phi_hi, phi_lo)
        hi, lo = split(mine * factor)
        pair = jnp.concatenate([hi, lo], axis=0)
        both = dot_nt(pair, phi_hi[...])
        return both[:BLK] + both[BLK:] + dot_nt(hi, phi_lo[...])

    def visit(m, carry):
        results = product(2 * m, m, even_ref), product(2 * m + 1, m, odd_ref)
        for k in range(2):
            for j in range(NBLK):
                total[:, columns_of(plan, 2 * m + k, j)] += results[k][:, j * BLK : (j + 1) * BLK]
        return carry

    lax.fori_loop(0, pairs, visit, 0)
    for i in range(4):
        at = pl.multiple_of((piece ^ i) * 32, 32)
        (keep_ref, send_ref)[i % 2][i // 2] = total[pl.ds(at, 32), :]


smem = pl.BlockSpec(memory_space=pltpu.SMEM)
vmem = pl.BlockSpec(memory_space=pltpu.VMEM)


def params(mib):
    return pltpu.CompilerParams(vmem_limit_bytes=mib << 20)


def held(x):
    return pltpu.with_memory_space_constraint(x, pltpu.VMEM)


def left(x):
    return pltpu.with_memory_space_constraint(x, pltpu.HBM)


def build(crowded, gathered, func, own_rows, near, far, cross):
    first, rest, even, odd, plan, count = pl.pallas_call(
        rho_kernel,
        out_shape=[
            pltpu.VMEM((OWNERS, KEPT * NBLK, BLK), jnp.float32),
            pltpu.VMEM((OWNERS, (SLOTS - KEPT) * NBLK, BLK), jnp.float32),
            pltpu.VMEM((SLOTS // 2, 2, PTS, PTS), jnp.bfloat16),
            pltpu.VMEM((SLOTS // 2, 2, PTS, PTS), jnp.bfloat16),
            jax.ShapeDtypeStruct(((SLOTS + 1) * STEP,), jnp.int32),
            jax.ShapeDtypeStruct((1,), jnp.int32),
        ],
        in_specs=[vmem] * 6,
        out_specs=[vmem] * 4 + [smem] * 2,
        scratch_shapes=[
            pltpu.VMEM((2 * BLK, NF), jnp.bfloat16),
            pltpu.VMEM((SLOTS // 2, FEAT, PTS), jnp.bfloat16),
            pltpu.VMEM((OWNERS * SLOTS * NBLK, BLK), jnp.float32),
            pltpu.SMEM((OWNERS, PACK - PTS), jnp.float32),
            pltpu.SMEM((OWNERS,), jnp.int32),
            pltpu.SemaphoreType.DMA((OWNERS,)),
        ],
        compiler_params=params(6),
        name="rho",
    )(held(gathered), held(func), held(own_rows), held(near), held(far), held(cross))
    parts = lax.all_to_all(first, "zh", 0, 0)
    others = lax.all_to_all(rest, "zh", 0, 0) if crowded else rest
    return pl.pallas_call(
        matrix_kernel,
        out_shape=[pltpu.VMEM((2, 32, NF), jnp.float32)] * 2,
        in_specs=[vmem] * 5 + [smem] * 2,
        out_specs=[vmem] * 2,
        scratch_shapes=[
            pltpu.VMEM((BLK, NF), jnp.float32),
            pltpu.VMEM((OWNERS * SLOTS * NBLK, BLK), jnp.float32),
            pltpu.VMEM((SLOTS, PTS), jnp.float32),
        ],
        compiler_params=params(4),
        name="matrix",
    )(held(gathered), held(parts), held(others), held(even), held(odd), plan, count)


def body(density, atom_xyz, atom_of, exponent, points, weights, lists, live):
    own_rows = density[0]
    packed = pl.pallas_call(
        pack_kernel,
        out_shape=pltpu.VMEM((OWNERS, 8, PACK), jnp.float32),
        in_specs=[pl.BlockSpec(memory_space=pl.ANY)] * 4,
        out_specs=vmem,
        scratch_shapes=[
            pltpu.VMEM((3, 2, PTS), jnp.float32),
            pltpu.VMEM((2, PTS), jnp.float32),
            pltpu.SMEM((2, NBLK), jnp.int32),
            pltpu.SMEM((1,), jnp.int32),
            pltpu.SemaphoreType.DMA((4,)),
        ],
        compiler_params=params(2),
        name="pack",
    )(left(jnp.transpose(points, (1, 0, 2))), left(weights), left(lists), live)
    gathered = lax.all_to_all(packed, "zh", 0, 0).reshape(SLOTS * 4, PACK)
    far = lax.ppermute(own_rows, "zl", SWAP)
    near = lax.ppermute(own_rows, "core", SWAP)
    func = pl.pallas_call(
        prep_kernel,
        out_shape=pltpu.VMEM((2, NF, FEAT), jnp.bfloat16),
        in_specs=[vmem] * 3,
        out_specs=vmem,
        compiler_params=params(8),
        cost_estimate=pl.CostEstimate(flops=4_000_000_000, bytes_accessed=1_000_000, transcendentals=0),
        name="prep",
    )(left(jnp.transpose(atom_xyz, (1, 0, 2))), left(atom_of), left(exponent))
    far, func = lax.optimization_barrier((far, func))
    cross = lax.ppermute(far, "core", SWAP)
    crowd = pl.pallas_call(
        crowd_kernel,
        out_shape=jax.ShapeDtypeStruct((1,), jnp.int32),
        in_specs=[vmem],
        out_specs=smem,
        compiler_params=params(2),
        name="crowd",
    )(held(gathered))
    keep, send = lax.cond(
        crowd[0] > 0,
        functools.partial(build, True),
        functools.partial(build, False),
        held(gathered), held(func), held(own_rows), held(near), held(far), held(cross),
    )
    got = lax.ppermute(send, "core", SWAP)
    other = lax.ppermute(keep[1] + got[1], "zl", SWAP)
    return (keep[0] + got[0] + other)[None]


def solution(mesh):
    torus = Mesh(mesh.devices.reshape(mesh.shape["region"], OWNERS, 2, 2), ALL)
    return jax.shard_map(
        body,
        mesh=torus,
        in_specs=(
            P("region", TILE, None),
            P("region", None, None),
            P("region", None),
            P("region", None),
            P(ALL, None, None),
            P(ALL, None),
            P(ALL, None),
            P(ALL),
        ),
        out_specs=P("region", TILE, None),
        check_vma=False,
    )
```

```python
import functools
import math

import jax
import jax.numpy as jnp
from jax import lax
from jax.experimental import pallas as pl
from jax.experimental.pallas import tpu as pltpu
from jax.sharding import Mesh
from jax.sharding import PartitionSpec as P

BLK = 128
NBLK = 4
PTS = 512
NF = 1024
OWNERS = 8
SLOTS = 16
PACK = 8 * 512 + 128
LIST = 8 * 512
FEAT = 64
KEPT = 10
STEP = 16
MID = 1.5
TILE = ("zh", "zl", "core")
ALL = ("region", "zh", "zl", "core")
SWAP = [(0, 1), (1, 0)]

slater_coef = (3.0 / math.pi) ** (1.0 / 3.0)


def split(x):
    hi = x.astype(jnp.bfloat16)
    lo = (x - hi.astype(jnp.float32)).astype(jnp.bfloat16)
    return hi, lo


def dot_nn(a, b):
    return lax.dot_general(a, b, (((1,), (0,)), ((), ())), preferred_element_type=jnp.float32)


def dot_nt(a, b):
    return lax.dot_general(a, b, (((1,), (1,)), ((), ())), preferred_element_type=jnp.float32)


def split3(x):
    first = x.astype(jnp.bfloat16).astype(jnp.float32)
    rest = x - first
    second = rest.astype(jnp.bfloat16).astype(jnp.float32)
    return first, second, rest - second


def list_copies(grid_ref, lists_f, sems):
    return [
        pltpu.make_async_copy(grid_ref.at[k, :, LIST:PACK], lists_f.at[k : k + 1], sems.at[k])
        for k in range(OWNERS)
    ]


def make_plan(lists_f, own, plan, seen):
    own_f = own.astype(jnp.float32)
    for k in range(OWNERS):
        seen[k] = 0
    n = jnp.int32(0)
    for b in range(SLOTS):
        listed = [lists_f[b // 2, (b % 2) * NBLK + j] for j in range(NBLK)]
        at = jnp.int32(0)
        named = jnp.int32(0)
        for j in range(NBLK):
            same = listed[j] == own_f
            at = jnp.where(same, j, at)
            named = jnp.where(same, 1, named)
        row = n * STEP
        plan[row] = jnp.int32(b)
        plan[row + 9] = at
        for j in range(NBLK):
            block = jnp.maximum(listed[j].astype(jnp.int32), 0)
            plan[row + 1 + j] = block
            rank = seen[block]
            plan[row + 5 + j] = rank
            seen[block] = rank + named
        n = n + named
    last = jnp.maximum(n - 1, 0) * STEP
    for k in range(10):
        plan[n * STEP + k] = plan[last + k]
    return n


def crowd_kernel(grid_ref, crowd_ref):
    lists = jnp.concatenate([grid_ref[k, :, LIST:PACK] for k in range(OWNERS)], axis=0)
    lane = lax.broadcasted_iota(jnp.int32, (OWNERS, BLK), 1).astype(jnp.float32)
    most = jnp.zeros((1, BLK), jnp.float32)
    marks = []
    for s in range(2):
        mark = jnp.zeros((OWNERS, BLK), jnp.float32)
        for j in range(NBLK):
            mark = jnp.where(lists[:, s * NBLK + j : s * NBLK + j + 1] == lane, 1.0, mark)
        marks.append(mark)
    for k in range(OWNERS):
        both = sum(mark * mark[:, k : k + 1] for mark in marks)
        total = jnp.sum(both, axis=0, keepdims=True)
        most = jnp.maximum(most, jnp.where(lane[0:1] == k, 0.0, total))
    crowd_ref[0] = (jnp.max(most) > KEPT).astype(jnp.int32)


def columns_of(plan, i, j):
    return pl.ds(pl.multiple_of(plan[i * STEP + 1 + j] * BLK, BLK), BLK)


def fill_phi(plan, i, func_ref, feat, phi_hi, phi_lo):
    b = plan[i * STEP]
    here = feat[b // 2]
    for j in range(NBLK):
        power = dot_nn(func_ref[b % 2, columns_of(plan, i, j), :], here)
        hi, lo = split(jnp.exp(power))
        phi_hi[j * BLK : (j + 1) * BLK, :] = hi
        phi_lo[j * BLK : (j + 1) * BLK, :] = lo


def own_phi(at, phi_hi, phi_lo):
    where = pl.ds(pl.multiple_of(at * BLK, BLK), BLK)
    return phi_hi[where, :].astype(jnp.float32) + phi_lo[where, :].astype(jnp.float32)


def pack_kernel(points_any, weights_any, lists_any, live_any, packed_ref, points_ref, weights_ref, lists_ref, live_ref, sems):
    pairs = ((points_any, points_ref), (weights_any, weights_ref), (lists_any, lists_ref), (live_any, live_ref))
    copies = [pltpu.make_async_copy(pair[0], pair[1], sems.at[i]) for i, pair in enumerate(pairs)]
    for copy in copies:
        copy.start()
    for copy in copies:
        copy.wait()
    rows = []
    for s in range(2):
        rows += [points_ref[c, s : s + 1, :] for c in range(3)] + [weights_ref[s : s + 1, :]]
    count = live_ref[0]
    lane = lax.broadcasted_iota(jnp.int32, (1, BLK), 1)
    extra = jnp.full((1, BLK), -1.0, jnp.float32)
    for s in range(2):
        for j in range(NBLK):
            named = jnp.where(s < count, lists_ref[s, j], -1).astype(jnp.float32)
            extra = jnp.where(lane == s * NBLK + j, named, extra)
    line = jnp.concatenate(rows + [extra], axis=1)
    for k in range(OWNERS):
        packed_ref[k] = line


def prep_kernel(xyz_ref, atom_ref, exp_ref, func_ref):
    atoms = lax.broadcasted_iota(jnp.int32, (256, NF), 0)
    picked = jnp.where(atoms == atom_ref[...], 1.0, 0.0).astype(jnp.bfloat16)
    parts = split3(jnp.concatenate([xyz_ref[c] for c in range(3)], axis=0) - MID)
    rows = jnp.concatenate([*parts, jnp.zeros((7, 256), jnp.float32)], axis=0)
    found = dot_nn(rows.astype(jnp.bfloat16), picked)
    x, y, z = (found[c : c + 1] + found[c + 3 : c + 4] + found[c + 6 : c + 7] for c in range(3))
    rate = exp_ref[...]
    twice = 2.0 * rate
    s1, s2, s3 = split3(jnp.concatenate([twice * x, twice * y, twice * z, -rate], axis=0))
    c1, c2, c3 = split3(-rate * (x * x + y * y + z * z))
    blank = jnp.zeros((4, NF), jnp.float32)
    side = []
    for part in (s1, s1, s2, s2, s1, s3):
        side += [part, blank]
    side += [c1, c2, c3, jnp.zeros((FEAT - 51, NF), jnp.float32)]
    columns = jnp.transpose(jnp.concatenate(side, axis=0))
    func_ref[0] = columns.astype(jnp.bfloat16)
    func_ref[1] = pltpu.roll(columns, 4, 1).astype(jnp.bfloat16)


def build_features(grid_ref, feat):
    lines = [grid_ref[k, :, c * PTS : (c + 1) * PTS] for k in range(OWNERS) for c in range(8)]
    centered = jnp.concatenate(lines, axis=0) - MID
    square = centered * centered
    norm = pltpu.roll(square, 1, 0) + pltpu.roll(square, 2, 0) + pltpu.roll(square, 3, 0)
    row = lax.broadcasted_iota(jnp.int32, (SLOTS * 4, PTS), 0)
    w1, w2, w3 = split3(jnp.where((row & 3) == 3, norm, centered))
    ones = jnp.ones((8, PTS), jnp.float32)
    for t in range(SLOTS // 2):
        at = slice(8 * t, 8 * t + 8)
        side = [part[at] for part in (w1, w2, w1, w2, w3, w1)] + [ones, ones]
        feat[t] = jnp.concatenate(side, axis=0).astype(jnp.bfloat16)


def rho_kernel(
    grid_ref, func_ref, d0, d1, d2, d3, first_ref, rest_ref, even_ref, odd_ref, plan, count_ref,
    dens, feat, rows, lists_f, seen, sems
):
    own = lax.axis_index("zh")
    piece = lax.axis_index("zl") * 2 + lax.axis_index("core")
    copies = list_copies(grid_ref, lists_f, sems)
    for copy in copies:
        copy.start()
    build_features(grid_ref, feat)
    for copy in copies:
        copy.wait()
    for i, ref in enumerate((d0, d1, d2, d3)):
        hi, lo = split(ref[...])
        at = pl.multiple_of((piece ^ i) * 32, 32)
        dens[pl.ds(at, 32), :] = hi
        dens[pl.ds(at + BLK, 32), :] = lo
    rows[...] = jnp.zeros_like(rows)
    count = make_plan(lists_f, own, plan, seen)
    count_ref[0] = count

    def make_phi(i, m, ref):
        fill_phi(plan, i, func_ref, feat, ref.at[m, 0], ref.at[m, 1])

    def make_rho(i, m, ref):
        phi_hi, phi_lo = ref.at[m, 0], ref.at[m, 1]
        mixed = jnp.zeros((BLK, PTS), jnp.float32)
        for j in range(0, NBLK, 2):
            pair = jnp.concatenate([dens[:, columns_of(plan, i, j + k)] for k in range(2)], axis=1)
            part = slice(j * BLK, (j + 2) * BLK)
            both = dot_nn(pair, phi_hi[part, :])
            mixed = mixed + both[:BLK] + both[BLK:] + dot_nn(pair[:BLK], phi_lo[part, :])
        mine = own_phi(plan[i * STEP + 9], phi_hi, phi_lo)
        total = jnp.sum(mine * mixed, axis=0, keepdims=True)
        for j in range(NBLK):
            at = plan[i * STEP + 1 + j] * (SLOTS * NBLK) + plan[i * STEP + 5 + j] * NBLK
            for t in range(PTS // BLK):
                rows[pl.ds(at + t, 1), :] = total[:, t * BLK : (t + 1) * BLK]

    pairs = (count + 1) // 2

    def visit(m, carry):
        before = jnp.maximum(m - 1, 0)
        make_phi(2 * m, m, even_ref)
        make_rho(2 * before + 1, before, odd_ref)
        make_phi(2 * m + 1, m, odd_ref)
        make_rho(2 * m, m, even_ref)
        return carry

    lax.fori_loop(0, pairs, visit, 0)

    @pl.when(pairs > 0)
    def _():
        make_rho(2 * pairs - 1, pairs - 1, odd_ref)

    for k in range(OWNERS):
        at = k * SLOTS * NBLK
        first_ref[k] = rows[at : at + KEPT * NBLK, :]
        rest_ref[k] = rows[at + KEPT * NBLK : at + SLOTS * NBLK, :]


def cube_root(x):
    size = jnp.abs(x)
    safe = jnp.maximum(size, 1e-37)
    y = jnp.exp(jnp.log(safe) * (1.0 / 3.0))
    y = y - (y - safe / (y * y)) * (1.0 / 3.0)
    y = jnp.where(size < 1e-37, 0.0, y)
    return jnp.where(x < 0.0, -y, y)


def matrix_kernel(
    grid_ref, first_ref, rest_ref, even_ref, odd_ref, plan, count_ref, keep_ref, send_ref, total, parts, root
):
    piece = lax.axis_index("zl") * 2 + lax.axis_index("core")
    count = count_ref[0]
    pairs = (count + 1) // 2

    for k in range(OWNERS):
        at = k * SLOTS * NBLK
        parts[at : at + KEPT * NBLK, :] = first_ref[k]
        parts[at + KEPT * NBLK : at + SLOTS * NBLK, :] = rest_ref[k]
    root[...] = jnp.zeros_like(root)
    total[...] = jnp.zeros_like(total)

    def gather(i, carry):
        at = [plan[i * STEP + 1 + j] * (SLOTS * NBLK) + plan[i * STEP + 5 + j] * NBLK for j in range(NBLK)]
        sums = [sum(parts[pl.ds(at[j] + t, 1), :] for j in range(NBLK)) for t in range(PTS // BLK)]
        root[pl.ds(i, 1), :] = jnp.concatenate(sums, axis=1)
        return carry

    lax.fori_loop(0, count, gather, 0)
    root[...] = cube_root(root[...]) * (-slater_coef)

    def product(i, at, ref):
        phi_hi, phi_lo = ref.at[at, 0], ref.at[at, 1]
        b = plan[i * STEP]
        lanes = pl.ds(pl.multiple_of((b % 2) * (4 * PTS) + 3 * PTS, BLK), PTS)
        factor = grid_ref[b // 2, :, lanes] * root[pl.ds(jnp.minimum(i, SLOTS - 1), 1), :]
        factor = jnp.where(i < count, factor, 0.0)
        mine = own_phi(plan[i * STEP + 9], phi_hi, phi_lo)
        hi, lo = split(mine * factor)
        pair = jnp.concatenate([hi, lo], axis=0)
        both = dot_nt(pair, phi_hi[...])
        return both[:BLK] + both[BLK:] + dot_nt(hi, phi_lo[...])

    def visit(m, carry):
        results = product(2 * m, m, even_ref), product(2 * m + 1, m, odd_ref)
        for k in range(2):
            for j in range(NBLK):
                total[:, columns_of(plan, 2 * m + k, j)] += results[k][:, j * BLK : (j + 1) * BLK]
        return carry

    lax.fori_loop(0, pairs, visit, 0)
    for i in range(4):
        at = pl.multiple_of((piece ^ i) * 32, 32)
        (keep_ref, send_ref)[i % 2][i // 2] = total[pl.ds(at, 32), :]


smem = pl.BlockSpec(memory_space=pltpu.SMEM)
vmem = pl.BlockSpec(memory_space=pltpu.VMEM)


def params(mib):
    return pltpu.CompilerParams(vmem_limit_bytes=mib << 20)


def held(x):
    return pltpu.with_memory_space_constraint(x, pltpu.VMEM)


def left(x):
    return pltpu.with_memory_space_constraint(x, pltpu.HBM)


def build(crowded, gathered, func, own_rows, near, far, cross):
    first, rest, even, odd, plan, count = pl.pallas_call(
        rho_kernel,
        out_shape=[
            pltpu.VMEM((OWNERS, KEPT * NBLK, BLK), jnp.float32),
            pltpu.VMEM((OWNERS, (SLOTS - KEPT) * NBLK, BLK), jnp.float32),
            pltpu.VMEM((SLOTS // 2, 2, PTS, PTS), jnp.bfloat16),
            pltpu.VMEM((SLOTS // 2, 2, PTS, PTS), jnp.bfloat16),
            jax.ShapeDtypeStruct(((SLOTS + 1) * STEP,), jnp.int32),
            jax.ShapeDtypeStruct((1,), jnp.int32),
        ],
        in_specs=[vmem] * 6,
        out_specs=[vmem] * 4 + [smem] * 2,
        scratch_shapes=[
            pltpu.VMEM((2 * BLK, NF), jnp.bfloat16),
            pltpu.VMEM((SLOTS // 2, FEAT, PTS), jnp.bfloat16),
            pltpu.VMEM((OWNERS * SLOTS * NBLK, BLK), jnp.float32),
            pltpu.SMEM((OWNERS, BLK), jnp.float32),
            pltpu.SMEM((OWNERS,), jnp.int32),
            pltpu.SemaphoreType.DMA((OWNERS,)),
        ],
        compiler_params=params(6),
        name="rho",
    )(held(gathered), held(func), held(own_rows), held(near), held(far), held(cross))
    parts = lax.all_to_all(first, "zh", 0, 0)
    others = lax.all_to_all(rest, "zh", 0, 0) if crowded else rest
    return pl.pallas_call(
        matrix_kernel,
        out_shape=[pltpu.VMEM((2, 32, NF), jnp.float32)] * 2,
        in_specs=[vmem] * 5 + [smem] * 2,
        out_specs=[vmem] * 2,
        scratch_shapes=[
            pltpu.VMEM((BLK, NF), jnp.float32),
            pltpu.VMEM((OWNERS * SLOTS * NBLK, BLK), jnp.float32),
            pltpu.VMEM((SLOTS, PTS), jnp.float32),
        ],
        compiler_params=params(4),
        name="matrix",
    )(held(gathered), held(parts), held(others), held(even), held(odd), plan, count)


def body(density, atom_xyz, atom_of, exponent, points, weights, lists, live):
    own_rows = density[0]
    packed = pl.pallas_call(
        pack_kernel,
        out_shape=pltpu.VMEM((OWNERS, 1, PACK), jnp.float32),
        in_specs=[pl.BlockSpec(memory_space=pl.ANY)] * 4,
        out_specs=vmem,
        scratch_shapes=[
            pltpu.VMEM((3, 2, PTS), jnp.float32),
            pltpu.VMEM((2, PTS), jnp.float32),
            pltpu.SMEM((2, NBLK), jnp.int32),
            pltpu.SMEM((1,), jnp.int32),
            pltpu.SemaphoreType.DMA((4,)),
        ],
        compiler_params=params(2),
        name="pack",
    )(left(jnp.transpose(points, (1, 0, 2))), left(weights), left(lists), live)
    gathered = lax.all_to_all(packed, "zh", 0, 0)
    far = lax.ppermute(own_rows, "zl", SWAP)
    near = lax.ppermute(own_rows, "core", SWAP)
    func = pl.pallas_call(
        prep_kernel,
        out_shape=pltpu.VMEM((2, NF, FEAT), jnp.bfloat16),
        in_specs=[vmem] * 3,
        out_specs=vmem,
        compiler_params=params(8),
        cost_estimate=pl.CostEstimate(flops=4_000_000_000, bytes_accessed=1_000_000, transcendentals=0),
        name="prep",
    )(left(jnp.transpose(atom_xyz, (1, 0, 2))), left(atom_of), left(exponent))
    far, func = lax.optimization_barrier((far, func))
    cross = lax.ppermute(far, "core", SWAP)
    crowd = pl.pallas_call(
        crowd_kernel,
        out_shape=pltpu.SMEM((1,), jnp.int32),
        in_specs=[vmem],
        out_specs=smem,
        compiler_params=params(2),
        name="crowd",
    )(held(gathered))
    keep, send = lax.cond(
        crowd[0] > 0,
        functools.partial(build, True),
        functools.partial(build, False),
        held(gathered), held(func), held(own_rows), held(near), held(far), held(cross),
    )
    got = lax.ppermute(send, "core", SWAP)
    other = lax.ppermute(keep[1] + got[1], "zl", SWAP)
    return (keep[0] + got[0] + other)[None]


def solution(mesh):
    torus = Mesh(mesh.devices.reshape(mesh.shape["region"], OWNERS, 2, 2), ALL)
    return jax.shard_map(
        body,
        mesh=torus,
        in_specs=(
            P("region", TILE, None),
            P("region", None, None),
            P("region", None),
            P("region", None),
            P(ALL, None, None),
            P(ALL, None),
            P(ALL, None),
            P(ALL),
        ),
        out_specs=P("region", TILE, None),
        check_vma=False,
    )
```

```python
import functools
import math

import jax
import jax.numpy as jnp
from jax import lax
from jax.experimental import pallas as pl
from jax.experimental.pallas import tpu as pltpu
from jax.sharding import Mesh
from jax.sharding import PartitionSpec as P


BLK = 128
NBLK = 4
PTS = 512
NF = 1024
OWNERS = 8
SLOTS = 16
PACK = 8 * 512 + 128
LIST = 8 * 512
FEAT = 64
KEPT = 10
STEP = 16
MID = 1.5
TILE = ("zh", "zl", "core")
ALL = ("region", "zh", "zl", "core")
SWAP = [(0, 1), (1, 0)]

slater_coef = (3.0 / math.pi) ** (1.0 / 3.0)


def split(x):
    hi = x.astype(jnp.bfloat16)
    lo = (x - hi.astype(jnp.float32)).astype(jnp.bfloat16)
    return hi, lo


def dot_nn(a, b):
    return lax.dot_general(a, b, (((1,), (0,)), ((), ())), preferred_element_type=jnp.float32)


def dot_nt(a, b):
    return lax.dot_general(a, b, (((1,), (1,)), ((), ())), preferred_element_type=jnp.float32)


def split3(x):
    first = x.astype(jnp.bfloat16).astype(jnp.float32)
    rest = x - first
    second = rest.astype(jnp.bfloat16).astype(jnp.float32)
    return first, second, rest - second


def list_copies(grid_ref, lists_f, sems):
    return [
        pltpu.make_async_copy(grid_ref.at[k, :, LIST:PACK], lists_f.at[k : k + 1], sems.at[k])
        for k in range(OWNERS)
    ]


def make_plan(lists_f, own, plan, seen):
    own_f = own.astype(jnp.float32)
    for k in range(OWNERS):
        seen[k] = 0
    n = jnp.int32(0)
    for b in range(SLOTS):
        listed = [lists_f[b // 2, (b % 2) * NBLK + j] for j in range(NBLK)]
        at = jnp.int32(0)
        named = jnp.int32(0)
        for j in range(NBLK):
            same = listed[j] == own_f
            at = jnp.where(same, j, at)
            named = jnp.where(same, 1, named)
        row = n * STEP
        plan[row] = jnp.int32(b)
        plan[row + 9] = at
        for j in range(NBLK):
            block = jnp.maximum(listed[j].astype(jnp.int32), 0)
            plan[row + 1 + j] = block
            rank = seen[block]
            plan[row + 5 + j] = rank
            seen[block] = rank + named
        n = n + named
    last = jnp.maximum(n - 1, 0) * STEP
    for k in range(10):
        plan[n * STEP + k] = plan[last + k]
    return n


def crowd_kernel(grid_ref, crowd_ref):
    lists = jnp.concatenate([grid_ref[k, :, LIST:PACK] for k in range(OWNERS)], axis=0)
    lane = lax.broadcasted_iota(jnp.int32, (OWNERS, BLK), 1).astype(jnp.float32)
    most = jnp.zeros((1, BLK), jnp.float32)
    marks = []
    for s in range(2):
        mark = jnp.zeros((OWNERS, BLK), jnp.float32)
        for j in range(NBLK):
            mark = jnp.where(lists[:, s * NBLK + j : s * NBLK + j + 1] == lane, 1.0, mark)
        marks.append(mark)
    for k in range(OWNERS):
        both = sum(mark * mark[:, k : k + 1] for mark in marks)
        total = jnp.sum(both, axis=0, keepdims=True)
        most = jnp.maximum(most, jnp.where(lane[0:1] == k, 0.0, total))
    crowd_ref[0] = (jnp.max(most) > KEPT).astype(jnp.int32)


def columns_of(plan, i, j):
    return pl.ds(pl.multiple_of(plan[i * STEP + 1 + j] * BLK, BLK), BLK)


def fill_phi(plan, i, func_ref, feat, phi_hi, phi_lo):
    b = plan[i * STEP]
    here = feat[b // 2]
    for j in range(NBLK):
        power = dot_nn(func_ref[b % 2, columns_of(plan, i, j), :], here)
        hi, lo = split(jnp.exp(power))
        phi_hi[j * BLK : (j + 1) * BLK, :] = hi
        phi_lo[j * BLK : (j + 1) * BLK, :] = lo


def own_phi(at, phi_hi, phi_lo):
    where = pl.ds(pl.multiple_of(at * BLK, BLK), BLK)
    return phi_hi[where, :].astype(jnp.float32) + phi_lo[where, :].astype(jnp.float32)


def pack_kernel(points_any, weights_any, lists_any, live_any, packed_ref, points_ref, weights_ref, lists_ref, live_ref, sems):
    pairs = ((points_any, points_ref), (weights_any, weights_ref), (lists_any, lists_ref), (live_any, live_ref))
    copies = [pltpu.make_async_copy(pair[0], pair[1], sems.at[i]) for i, pair in enumerate(pairs)]
    for copy in copies:
        copy.start()
    for copy in copies:
        copy.wait()
    rows = []
    for s in range(2):
        rows += [points_ref[c, s : s + 1, :] for c in range(3)] + [weights_ref[s : s + 1, :]]
    count = live_ref[0]
    lane = lax.broadcasted_iota(jnp.int32, (1, BLK), 1)
    extra = jnp.full((1, BLK), -1.0, jnp.float32)
    for s in range(2):
        for j in range(NBLK):
            named = jnp.where(s < count, lists_ref[s, j], -1).astype(jnp.float32)
            extra = jnp.where(lane == s * NBLK + j, named, extra)
    line = jnp.concatenate(rows + [extra], axis=1)
    for k in range(OWNERS):
        packed_ref[k] = line


def prep_kernel(xyz_ref, atom_ref, exp_ref, func_ref):
    atoms = lax.broadcasted_iota(jnp.int32, (256, NF), 0)
    picked = jnp.where(atoms == atom_ref[...], 1.0, 0.0).astype(jnp.bfloat16)
    parts = split3(jnp.concatenate([xyz_ref[c] for c in range(3)], axis=0) - MID)
    rows = jnp.concatenate([*parts, jnp.zeros((7, 256), jnp.float32)], axis=0)
    found = dot_nn(rows.astype(jnp.bfloat16), picked)
    x, y, z = (found[c : c + 1] + found[c + 3 : c + 4] + found[c + 6 : c + 7] for c in range(3))
    rate = exp_ref[...]
    twice = 2.0 * rate
    s1, s2, s3 = split3(jnp.concatenate([twice * x, twice * y, twice * z, -rate], axis=0))
    c1, c2, c3 = split3(-rate * (x * x + y * y + z * z))
    blank = jnp.zeros((4, NF), jnp.float32)
    side = []
    for part in (s1, s1, s2, s2, s1, s3):
        side += [part, blank]
    side += [c1, c2, c3, jnp.zeros((FEAT - 51, NF), jnp.float32)]
    columns = jnp.transpose(jnp.concatenate(side, axis=0))
    func_ref[0] = columns.astype(jnp.bfloat16)
    func_ref[1] = pltpu.roll(columns, 4, 1).astype(jnp.bfloat16)


def build_features(grid_ref, feat):
    lines = [grid_ref[k, :, c * PTS : (c + 1) * PTS] for k in range(OWNERS) for c in range(8)]
    centered = jnp.concatenate(lines, axis=0) - MID
    square = centered * centered
    norm = pltpu.roll(square, 1, 0) + pltpu.roll(square, 2, 0) + pltpu.roll(square, 3, 0)
    row = lax.broadcasted_iota(jnp.int32, (SLOTS * 4, PTS), 0)
    w1, w2, w3 = split3(jnp.where((row & 3) == 3, norm, centered))
    ones = jnp.ones((8, PTS), jnp.float32)
    for t in range(SLOTS // 2):
        at = slice(8 * t, 8 * t + 8)
        side = [part[at] for part in (w1, w2, w1, w2, w3, w1)] + [ones, ones]
        feat[t] = jnp.concatenate(side, axis=0).astype(jnp.bfloat16)


def rho_kernel(
    grid_ref, func_ref, own_rows, far_rows, both_rows, first_ref, rest_ref, even_ref, odd_ref, plan, count_ref,
    dens, feat, rows, lists_f, seen, sems
):
    own = lax.axis_index("zh")
    piece = lax.axis_index("zl") * 2 + lax.axis_index("core")
    copies = list_copies(grid_ref, lists_f, sems)
    for copy in copies:
        copy.start()
    build_features(grid_ref, feat)
    for copy in copies:
        copy.wait()
    for i, ref in enumerate((own_rows, both_rows.at[0], far_rows, both_rows.at[1])):
        hi, lo = split(ref[...])
        at = pl.multiple_of((piece ^ i) * 32, 32)
        dens[pl.ds(at, 32), :] = hi
        dens[pl.ds(at + BLK, 32), :] = lo
    rows[...] = jnp.zeros_like(rows)
    count = make_plan(lists_f, own, plan, seen)
    count_ref[0] = count

    def make_phi(i, m, ref):
        fill_phi(plan, i, func_ref, feat, ref.at[m, 0], ref.at[m, 1])

    def make_rho(i, m, ref):
        phi_hi, phi_lo = ref.at[m, 0], ref.at[m, 1]
        mixed = jnp.zeros((BLK, PTS), jnp.float32)
        for j in range(0, NBLK, 2):
            pair = jnp.concatenate([dens[:, columns_of(plan, i, j + k)] for k in range(2)], axis=1)
            part = slice(j * BLK, (j + 2) * BLK)
            both = dot_nn(pair, phi_hi[part, :])
            mixed = mixed + both[:BLK] + both[BLK:] + dot_nn(pair[:BLK], phi_lo[part, :])
        mine = own_phi(plan[i * STEP + 9], phi_hi, phi_lo)
        total = jnp.sum(mine * mixed, axis=0, keepdims=True)
        for j in range(NBLK):
            at = plan[i * STEP + 1 + j] * (SLOTS * NBLK) + plan[i * STEP + 5 + j] * NBLK
            for t in range(PTS // BLK):
                rows[pl.ds(at + t, 1), :] = total[:, t * BLK : (t + 1) * BLK]

    pairs = (count + 1) // 2

    def visit(m, carry):
        before = jnp.maximum(m - 1, 0)
        make_phi(2 * m, m, even_ref)
        make_rho(2 * before + 1, before, odd_ref)
        make_phi(2 * m + 1, m, odd_ref)
        make_rho(2 * m, m, even_ref)
        return carry

    lax.fori_loop(0, pairs, visit, 0)

    @pl.when(pairs > 0)
    def _():
        make_rho(2 * pairs - 1, pairs - 1, odd_ref)

    for k in range(OWNERS):
        at = k * SLOTS * NBLK
        first_ref[k] = rows[at : at + KEPT * NBLK, :]
        rest_ref[k] = rows[at + KEPT * NBLK : at + SLOTS * NBLK, :]


def cube_root(x):
    size = jnp.abs(x)
    safe = jnp.maximum(size, 1e-37)
    y = jnp.exp(jnp.log(safe) * (1.0 / 3.0))
    y = y - (y - safe / (y * y)) * (1.0 / 3.0)
    y = jnp.where(size < 1e-37, 0.0, y)
    return jnp.where(x < 0.0, -y, y)


def matrix_kernel(
    grid_ref, first_ref, rest_ref, even_ref, odd_ref, plan, count_ref, keep_ref, send_ref, total, parts, root
):
    piece = lax.axis_index("zl") * 2 + lax.axis_index("core")
    count = count_ref[0]
    pairs = (count + 1) // 2

    for k in range(OWNERS):
        at = k * SLOTS * NBLK
        parts[at : at + KEPT * NBLK, :] = first_ref[k]
        parts[at + KEPT * NBLK : at + SLOTS * NBLK, :] = rest_ref[k]
    root[...] = jnp.zeros_like(root)
    total[...] = jnp.zeros_like(total)

    def gather(i, carry):
        at = [plan[i * STEP + 1 + j] * (SLOTS * NBLK) + plan[i * STEP + 5 + j] * NBLK for j in range(NBLK)]
        sums = [sum(parts[pl.ds(at[j] + t, 1), :] for j in range(NBLK)) for t in range(PTS // BLK)]
        root[pl.ds(i, 1), :] = jnp.concatenate(sums, axis=1)
        return carry

    lax.fori_loop(0, count, gather, 0)
    root[...] = cube_root(root[...]) * (-slater_coef)

    def product(i, at, ref):
        phi_hi, phi_lo = ref.at[at, 0], ref.at[at, 1]
        b = plan[i * STEP]
        lanes = pl.ds(pl.multiple_of((b % 2) * (4 * PTS) + 3 * PTS, BLK), PTS)
        factor = grid_ref[b // 2, :, lanes] * root[pl.ds(jnp.minimum(i, SLOTS - 1), 1), :]
        factor = jnp.where(i < count, factor, 0.0)
        mine = own_phi(plan[i * STEP + 9], phi_hi, phi_lo)
        hi, lo = split(mine * factor)
        pair = jnp.concatenate([hi, lo], axis=0)
        both = dot_nt(pair, phi_hi[...])
        return both[:BLK] + both[BLK:] + dot_nt(hi, phi_lo[...])

    def visit(m, carry):
        results = product(2 * m, m, even_ref), product(2 * m + 1, m, odd_ref)
        for k in range(2):
            for j in range(NBLK):
                total[:, columns_of(plan, 2 * m + k, j)] += results[k][:, j * BLK : (j + 1) * BLK]
        return carry

    lax.fori_loop(0, pairs, visit, 0)
    for i in range(4):
        at = pl.multiple_of((piece ^ i) * 32, 32)
        (keep_ref, send_ref)[i % 2][i // 2] = total[pl.ds(at, 32), :]


smem = pl.BlockSpec(memory_space=pltpu.SMEM)
vmem = pl.BlockSpec(memory_space=pltpu.VMEM)


def params(mib):
    return pltpu.CompilerParams(vmem_limit_bytes=mib << 20)


def held(x):
    return pltpu.with_memory_space_constraint(x, pltpu.VMEM)


def left(x):
    return pltpu.with_memory_space_constraint(x, pltpu.HBM)


def build(crowded, gathered, func, own_rows, far, both):
    first, rest, even, odd, plan, count = pl.pallas_call(
        rho_kernel,
        out_shape=[
            pltpu.VMEM((OWNERS, KEPT * NBLK, BLK), jnp.float32),
            pltpu.VMEM((OWNERS, (SLOTS - KEPT) * NBLK, BLK), jnp.float32),
            pltpu.VMEM((SLOTS // 2, 2, PTS, PTS), jnp.bfloat16),
            pltpu.VMEM((SLOTS // 2, 2, PTS, PTS), jnp.bfloat16),
            jax.ShapeDtypeStruct(((SLOTS + 1) * STEP,), jnp.int32),
            jax.ShapeDtypeStruct((1,), jnp.int32),
        ],
        in_specs=[vmem] * 5,
        out_specs=[vmem] * 4 + [smem] * 2,
        scratch_shapes=[
            pltpu.VMEM((2 * BLK, NF), jnp.bfloat16),
            pltpu.VMEM((SLOTS // 2, FEAT, PTS), jnp.bfloat16),
            pltpu.VMEM((OWNERS * SLOTS * NBLK, BLK), jnp.float32),
            pltpu.SMEM((OWNERS, BLK), jnp.float32),
            pltpu.SMEM((OWNERS,), jnp.int32),
            pltpu.SemaphoreType.DMA((OWNERS,)),
        ],
        compiler_params=params(6),
        name="rho",
    )(held(gathered), held(func), held(own_rows), held(far), held(both))
    parts = lax.all_to_all(first, "zh", 0, 0)
    others = lax.all_to_all(rest, "zh", 0, 0) if crowded else rest
    return pl.pallas_call(
        matrix_kernel,
        out_shape=[pltpu.VMEM((2, 32, NF), jnp.float32)] * 2,
        in_specs=[vmem] * 5 + [smem] * 2,
        out_specs=[vmem] * 2,
        scratch_shapes=[
            pltpu.VMEM((BLK, NF), jnp.float32),
            pltpu.VMEM((OWNERS * SLOTS * NBLK, BLK), jnp.float32),
            pltpu.VMEM((SLOTS, PTS), jnp.float32),
        ],
        compiler_params=params(4),
        name="matrix",
    )(held(gathered), held(parts), held(others), held(even), held(odd), plan, count)


def body(density, atom_xyz, atom_of, exponent, points, weights, lists, live):
    own_rows = density[0]
    packed = pl.pallas_call(
        pack_kernel,
        out_shape=pltpu.VMEM((OWNERS, 1, PACK), jnp.float32),
        in_specs=[pl.BlockSpec(memory_space=pl.ANY)] * 4,
        out_specs=vmem,
        scratch_shapes=[
            pltpu.VMEM((3, 2, PTS), jnp.float32),
            pltpu.VMEM((2, PTS), jnp.float32),
            pltpu.SMEM((2, NBLK), jnp.int32),
            pltpu.SMEM((1,), jnp.int32),
            pltpu.SemaphoreType.DMA((4,)),
        ],
        compiler_params=params(2),
        name="pack",
    )(left(jnp.transpose(points, (1, 0, 2))), left(weights), left(lists), live)
    gathered = lax.all_to_all(packed, "zh", 0, 0)
    far = lax.ppermute(own_rows, "zl", SWAP)
    func = pl.pallas_call(
        prep_kernel,
        out_shape=pltpu.VMEM((2, NF, FEAT), jnp.bfloat16),
        in_specs=[vmem] * 3,
        out_specs=vmem,
        compiler_params=params(8),
        cost_estimate=pl.CostEstimate(flops=4_000_000_000, bytes_accessed=1_000_000, transcendentals=0),
        name="prep",
    )(left(jnp.transpose(atom_xyz, (1, 0, 2))), left(atom_of), left(exponent))
    far, func = lax.optimization_barrier((far, func))
    both = lax.ppermute(jnp.stack([own_rows, far]), "core", SWAP)
    crowd = pl.pallas_call(
        crowd_kernel,
        out_shape=pltpu.SMEM((1,), jnp.int32),
        in_specs=[vmem],
        out_specs=smem,
        compiler_params=params(2),
        name="crowd",
    )(held(gathered))
    keep, send = lax.cond(
        crowd[0] > 0,
        functools.partial(build, True),
        functools.partial(build, False),
        held(gathered), held(func), held(own_rows), held(far), held(both),
    )
    got = lax.ppermute(send, "core", SWAP)
    other = lax.ppermute(keep[1] + got[1], "zl", SWAP)
    return (keep[0] + got[0] + other)[None]


def solution(mesh):
    torus = Mesh(mesh.devices.reshape(mesh.shape["region"], OWNERS, 2, 2), ALL)
    return jax.shard_map(
        body,
        mesh=torus,
        in_specs=(
            P("region", TILE, None),
            P("region", None, None),
            P("region", None),
            P("region", None),
            P(ALL, None, None),
            P(ALL, None),
            P(ALL, None),
            P(ALL),
        ),
        out_specs=P("region", TILE, None),
        check_vma=False,
    )
```
